256 devices in a mesh: kx: 32 (over x_hi, z, core), ky: 8 (over y, x_lo).
Axes of the slice: x: 4 (x_hi: 2, x_lo: 2; x = x_hi * 2 + x_lo), y: 4, z: 8, core: 2. Of those that a mesh axis runs over, the one named last changes fastest.
Arguments:
- waves: bfloat16 [2, 32, 16, 8, 1024], P(None, 'kx', 'ky'), may hold values from -0.8984375 to 0.8984375
- screened: bfloat16 [2, 2, 1024, 1024], P(None, None, 'kx'), may hold values from -0.005859375 to 0.005859375
- coulomb: float32 [1024], replicated, may hold values from 0.001 to 0.1
- transfers: int32 [2, 2], replicated, may hold values from 0 to 31, as said below
- gmap: int32 [2, 4, 1024], replicated, may hold values from 0 to 1023, as said below
Outputs:
- direct: float32 [2, 2, 32, 16, 256], P(None, None, 'kx', 'ky')
- exchange: float32 [2, 2, 32, 16, 256], P(None, None, 'kx', 'ky')
The draws below stay inside these ranges and needn't reach their ends.
Inputs may be any that keep to these rules, and one draw needn't show every extreme that they name: transfers[j, 0] lies in 0 to 31 and transfers[j, 1] in 0 to 15; transfers[0, 1] is 15 and transfers[1, 0] is 31. Each row gmap[j, case] holds 1024 distinct plane-wave indices of 0 to 1023, among them 0 and 1023.
All inputs are finite; a program needn't handle non-finite values.
Results may differ from the reference program's by a relative error of at most 0.0072.
Values may be sent and summed in bfloat16 or wider, within the bound.
A program may use at most 64 MiB of HBM per device.

```python
import math
import jax
import jax.numpy as jnp
from jax import lax

NV = 4
NC = 4
NB = 8
NG = 1024
NW = 1024
NR = 1024
NQ = 2
NKX = 32
NKY = 16


def draw_transfers(key, part):
    first_x = jax.random.randint(jax.random.fold_in(key, 11), (), 0, NKX)
    second_y = jax.random.randint(jax.random.fold_in(key, 12), (), 0, NKY)
    rows = jnp.stack([jnp.stack([first_x, jnp.int32(NKY - 1)]), jnp.stack([jnp.int32(NKX - 1), second_y])])
    return rows.astype(jnp.int32)


def draw_gmap(key, part):
    keys = jax.random.split(jax.random.fold_in(key, 17), NQ * 4)

    def one_row(row_key):
        inner_key = jax.random.fold_in(row_key, 1)
        order_key = jax.random.fold_in(row_key, 2)
        middle = jax.random.permutation(inner_key, NG - 2)[:NW - 2] + 1
        chosen = jnp.concatenate([jnp.array([0, NG - 1], dtype=jnp.int32), middle.astype(jnp.int32)])
        return jax.random.permutation(order_key, chosen)
    rows = jax.vmap(one_row)(keys)
    return rows.reshape(NQ, 4, NW).astype(jnp.int32)


def steps_of(stream_key, extent, shards, low, top_value):
    gain, own = 1.0, jax.random.fold_in(stream_key, 6)
    for position, shards_of in shards:
        steps = jnp.exp(jax.random.uniform(jax.random.fold_in(own, position), (shards_of,), jnp.float32, low / len(shards), top_value / len(shards)))
        gain = gain * jnp.repeat(steps, extent[position] // shards_of).reshape([-1 if axis == position else 1 for axis in range(len(extent))])
    return gain


def normal_values(key, extent, spread, limit, cuts=(), kind=jnp.bfloat16):
    loudness = steps_of(key, extent, cuts, -0.22, 0.18) if cuts else 1.0
    values = jax.random.normal(key, extent, jnp.float32) * spread * loudness
    return jnp.minimum(jnp.maximum(values, -limit), limit).astype(kind)


def setup_inputs(seed: int = 0) -> dict:
    splits = jax.random.split(jax.random.key(seed), 6)
    waves = normal_values(splits[0], (2, NKX, NKY, NB, NR), 0.15, 0.8984375, ((1, 32), (2, 8)))
    screened = normal_values(splits[1], (NQ, 2, NW, NW), (NW * NW) ** -0.5, 0.005859375, ((2, 32),))
    coulomb = jnp.clip(jnp.exp(jax.random.uniform(splits[2], (NG,), jnp.float32, math.log(0.001), math.log(0.1))), 0.001, 0.1)
    transfers = draw_transfers(jax.random.fold_in(splits[5], 71), 0)
    gmap = draw_gmap(jax.random.fold_in(splits[5], 71), 0)
    return dict(waves=waves, screened=screened, coulomb=coulomb, transfers=transfers, gmap=gmap)


block_rows = 256
full_turn = 2.0 * math.pi


def phase_table(freqs, grid):
    places = jnp.arange(grid, dtype=jnp.int32)
    turns = jnp.mod(freqs[:, None].astype(jnp.int32) * places[None, :], grid)
    angles = turns.astype(jnp.float32) * (full_turn / grid)
    return jnp.cos(angles).astype(jnp.bfloat16), jnp.sin(angles).astype(jnp.bfloat16)


def pair_terms(left, right):
    left_re = left[0].astype(jnp.float32)
    left_im = left[1].astype(jnp.float32)
    right_re = right[0].astype(jnp.float32)
    right_im = right[1].astype(jnp.float32)
    width = left.shape[-1]
    real_part = (left_re[:, None, :] * right_re[None, :, :] + left_im[:, None, :] * right_im[None, :, :]).reshape(-1, width)
    imag_part = (left_re[:, None, :] * right_im[None, :, :] - left_im[:, None, :] * right_re[None, :, :]).reshape(-1, width)
    return real_part, imag_part


def stack_pairs(terms):
    reals = jnp.concatenate([term[0] for term in terms], 0)
    imags = jnp.concatenate([term[1] for term in terms], 0)
    return jnp.concatenate([reals, imags], 0).astype(jnp.bfloat16)


def contract_last(left, right):
    return lax.dot_general(left.astype(jnp.float32), right.astype(jnp.float32), (((1,), (1,)), ((), ())), precision=lax.Precision.HIGHEST, preferred_element_type=jnp.float32)


def transform(stacked, freqs):
    grid = stacked.shape[1]
    count = stacked.shape[0] // 2
    width = min(block_rows, freqs.shape[0])

    def one_block(part):
        cosines, sines = phase_table(part, grid)
        with_cos = contract_last(stacked, cosines)
        with_sin = contract_last(stacked, sines)
        real_part = with_cos[:count] + with_sin[count:]
        imag_part = with_cos[count:] - with_sin[:count]
        return jnp.stack([real_part, imag_part]).astype(jnp.bfloat16)

    blocks = lax.map(one_block, freqs.reshape(-1, width))
    return jnp.transpose(blocks, (1, 2, 0, 3)).reshape(2, count, -1)


def kernel_parts(left, right):
    real_part = contract_last(left[0], right[0]) + contract_last(left[1], right[1])
    imag_part = contract_last(left[0], right[1]) - contract_last(left[1], right[0])
    return jnp.stack([real_part, imag_part])


def reference(waves, screened, coulomb, transfers, gmap):
    points = NKX * NKY
    flat = jnp.moveaxis(waves.reshape(2, points, NB, NR), 1, 0)
    own_freqs = jnp.arange(NG, dtype=jnp.int32) - NG // 2

    def exchange_density(single):
        return transform(stack_pairs([pair_terms(single[:, :NV], single[:, NV:])]), own_freqs)

    ex_dens = lax.map(exchange_density, flat)
    point_ids = jnp.arange(points, dtype=jnp.int32)
    first_ids = point_ids // NKY
    second_ids = point_ids % NKY
    direct_list = []
    exchange_list = []
    for which in range(NQ):
        trans_x = transfers[which, 0]
        trans_y = transfers[which, 1]
        target_ids = ((first_ids + trans_x) % NKX) * NKY + (second_ids + trans_y) % NKY
        cases = (first_ids + trans_x >= NKX).astype(jnp.int32) + 2 * (second_ids + trans_y >= NKY).astype(jnp.int32)
        real_w = screened[which, 0].astype(jnp.float32)
        imag_w = screened[which, 1].astype(jnp.float32)

        def per_point(index):
            here = flat[index]
            target = target_ids[index]
            there = flat[target]
            freq_row = gmap[which][cases[index]] - NG // 2
            stacked = stack_pairs([pair_terms(here[:, NV:], there[:, NV:]), pair_terms(here[:, :NV], there[:, :NV])])
            dens = transform(stacked, freq_row)
            cond_part = dens[:, :NC * NC]
            val_part = dens[:, NC * NC:].astype(jnp.float32)
            hp = lax.Precision.HIGHEST
            y_real = jnp.einsum("gh,ph->pg", real_w, val_part[0], precision=hp) - jnp.einsum("gh,ph->pg", imag_w, val_part[1], precision=hp)
            y_imag = jnp.einsum("gh,ph->pg", real_w, val_part[1], precision=hp) + jnp.einsum("gh,ph->pg", imag_w, val_part[0], precision=hp)
            screened_pairs = jnp.stack([y_real, y_imag]).astype(jnp.bfloat16)
            block = kernel_parts(cond_part, screened_pairs)
            block = block.reshape(2, NC, NC, NV, NV).transpose(0, 3, 1, 4, 2).reshape(2, -1)
            weighted = (ex_dens[target].astype(jnp.float32) * coulomb).astype(jnp.bfloat16)
            exch = kernel_parts(ex_dens[index], weighted).reshape(2, -1)
            return block, exch

        block_all, exch_all = lax.map(per_point, point_ids)
        direct_list.append(jnp.transpose(block_all.reshape(NKX, NKY, 2, -1), (2, 0, 1, 3)))
        exchange_list.append(jnp.transpose(exch_all.reshape(NKX, NKY, 2, -1), (2, 0, 1, 3)))
    return jnp.stack(direct_list), jnp.stack(exchange_list)
```

```python
import functools

import jax
import jax.numpy as jnp
import numpy as np
from jax import lax
from jax.experimental import pallas as pl
from jax.experimental.pallas import tpu as pltpu
from jax.sharding import PartitionSpec as P

MESH = pl.DeviceIdType.MESH
OFFS = (0, -1, 1, -2, 2, -3, 3, 4)
BF = jnp.bfloat16
F32 = jnp.float32
NT = (((1,), (1,)), ((), ()))


def table():
    r = np.arange(1024)
    turns = (r[:, None] * r[None, :512]) % 1024
    angles = turns.astype(np.float32) * np.float32(2.0 * np.pi / 1024)
    both = np.concatenate([np.cos(angles), np.sin(angles)], 1)
    return jnp.asarray(both, dtype=BF)


def dot(a, b):
    return lax.dot_general(a, b, (((1,), (0,)), ((), ())), preferred_element_type=F32)


def dot_nt(a, b):
    return lax.dot_general(a, b, NT, preferred_element_type=F32)


def kernel(
    transfers, here, there, scr, gmap, coulomb, tab, out,
    w, hb, tb, lhs, dens, hot, bl, ap, yb, zb, res,
    sem_loc, zs, zr, xds, xdr, xss, xsr, ss, sr,
):
    kx = lax.axis_index("kx")
    ky = lax.axis_index("ky")
    c = kx % 2
    m = kx // 2
    h = m // 8
    z = m % 8
    y = ky // 2
    xl = ky % 2

    def dev(h_, z_, c_, y_, xl_):
        return ((h_ * 8 + z_) * 2 + c_, y_ * 2 + xl_)

    up = dev(h, (z + 1) % 8, c, y, xl)
    down = dev(h, (z + 7) % 8, c, y, xl)
    cross = dev(1 - h, z, c, y, 1 - xl)
    side = dev(h, z, c, y, 1 - xl)
    sib = dev(h, z, 1 - c, y, xl)

    barrier = pltpu.get_barrier_semaphore()
    for d in (up, down, cross, side, sib):
        pl.semaphore_signal(barrier, inc=1, device_id=d, device_id_type=MESH)
    pl.semaphore_wait(barrier, 5)

    started = []

    def send(src, dst, s, r, d):
        cp = pltpu.make_async_remote_copy(
            src_ref=src, dst_ref=dst, send_sem=s, recv_sem=r, device_id=d, device_id_type=MESH
        )
        cp.start()
        started.append(cp)

    def zb_of(k):
        return (z + OFFS[k] + 8) % 8

    def half(hh, k, cc):
        return w.at[:, hh, zb_of(k), cc]

    own_w = pltpu.make_async_copy(scr.at[c], w.at[:, h, z, c], sem_loc.at[0])
    own_w.start()
    own_h = pltpu.make_async_copy(here, hb.at[0], sem_loc.at[1])
    own_h.start()
    own_t = pltpu.make_async_copy(there.at[c], tb.at[0], sem_loc.at[2])
    own_t.start()
    send(here, hb.at[1], ss.at[0], sr.at[0], sib)
    send(there.at[1 - c], tb.at[1], ss.at[1], sr.at[1], sib)
    send(scr.at[1 - c], w.at[:, h, z, c], ss.at[2], sr.at[2], sib)

    def landed(dst, r):
        pltpu.make_async_remote_copy(
            src_ref=dst, dst_ref=dst, send_sem=ss.at[0], recv_sem=r, device_id=sib, device_id_type=MESH
        ).wait_recv()

    def z_send(k, cc, n, d, k2):
        send(half(h, k, cc), half(h, k, cc), zs.at[n, cc], zr.at[k2, cc], d)

    def x_send(k):
        cc = 1 - xl
        send(half(h, k, cc), half(h, k, cc), xds.at[k], xdr.at[k], cross)

    def z_recv(k, cc):
        landed(half(h, k, cc), zr.at[k, cc])

    def side_step(k):
        landed(half(1 - h, k, xl), xdr.at[k])
        send(half(1 - h, k, xl), half(1 - h, k, xl), xss.at[k], xsr.at[k], side)

    own_w.wait()
    landed(w.at[:, h, z, 1 - c], sr.at[2])
    for cc in (0, 1):
        z_send(0, cc, 0, up, 1)
        z_send(0, cc, 1, down, 2)
    x_send(0)

    own_h.wait()
    own_t.wait()
    landed(hb.at[1], sr.at[0])
    landed(tb.at[1], sr.at[1])
    low = lax.broadcasted_iota(jnp.int32, (8, 1024), 0) < 4
    odd = lax.broadcasted_iota(jnp.int32, (8, 1024), 1) % 2 == 1
    sign = jnp.where(odd, F32(-1.0), F32(1.0))

    def left(x, first):
        rows = [jnp.broadcast_to(x[first + i : first + i + 1], (8, 1024)) for i in range(4)]
        return jnp.where(low, rows[0], rows[1]), jnp.where(low, rows[2], rows[3])

    def right(x):
        sw = pltpu.roll(x, 4, 0)
        return jnp.where(low, x, sw), jnp.where(low, sw, x)

    for q in range(4):
        p, pt = q // 2, q % 2
        hre = hb[p, 0, pt].astype(F32)
        him = hb[p, 1, pt].astype(F32)
        tre = tb[p, 0, pt].astype(F32)
        tim = tb[p, 1, pt].astype(F32)
        hv, hc = (left(hre, 0), left(him, 0)), (left(hre, 4), left(him, 4))
        tv = (left(tre, 0), left(tim, 0))
        (hrv, hrc), (hiv, hic) = right(hre), right(him)
        (trv, trc), (tiv, tic) = right(tre), right(tim)
        kinds = (
            (hc, trc, tic), (hv, trv, tiv), (hv, hrc, hic), (tv, trc, tic),
        )
        for t, ((lr, li), rr, ri) in enumerate(kinds):
            re = jnp.concatenate([lr[i] * rr + li[i] * ri for i in (0, 1)], 0)
            im = jnp.concatenate([lr[i] * ri - li[i] * rr for i in (0, 1)], 0)
            s2 = jnp.concatenate([sign, sign], 0)
            lhs[t, q * 16 : q * 16 + 16] = re.astype(BF)
            lhs[t, 64 + q * 16 : 80 + q * 16] = im.astype(BF)
            lhs[t, 128 + q * 16 : 144 + q * 16] = (re * s2).astype(BF)
            lhs[t, 192 + q * 16 : 208 + q * 16] = (im * s2).astype(BF)

    def round_z(ka, kb, na, nb):
        for cc in (0, 1):
            z_recv(ka, cc)
            if na is not None and (na[1] is None or cc in na[1]):
                z_send(ka, cc, na[0], up, na[2])
            z_recv(kb, cc)
            if nb is not None and (nb[1] is None or cc in nb[1]):
                z_send(kb, cc, nb[0], down, nb[2])
        x_send(ka)
        x_send(kb)

    def transform(t):
        for g in (0, 1):
            o = dot(lhs[t, g * 128 : g * 128 + 128], tab[...])
            cols = slice(512, 1024) if g == 0 else slice(0, 512)
            dens[t, :64, cols] = (o[:64, :512] + o[64:, 512:]).astype(BF)
            dens[t, 64:, cols] = (o[64:, :512] - o[:64, 512:]).astype(BF)

    transform(0)
    round_z(1, 2, (2, None, 3), (3, None, 4))
    side_step(0)
    transform(1)
    round_z(3, 4, (4, None, 5), (5, None, 6))
    side_step(1)
    side_step(2)

    def permute(q):
        p, pt = q // 2, q % 2
        core = jnp.where(p == 0, c, 1 - c)
        tx = transfers[c, 0]
        ty = transfers[c, 1]
        wx = jnp.where(m * 2 + core + tx >= 32, 1, 0)
        wy = jnp.where(ky * 2 + pt + ty >= 16, 2, 0)
        row = gmap[pl.ds(c * 4 + wx + wy, 1), :]
        hot[...] = jnp.where(
            lax.broadcasted_iota(jnp.int32, (1024, 1024), 0) == row, F32(1.0), F32(0.0)
        ).astype(BF)
        rows = jnp.concatenate(
            [
                dens[0, q * 16 : q * 16 + 16],
                dens[0, 64 + q * 16 : 80 + q * 16],
                dens[1, q * 16 : q * 16 + 16],
                dens[1, 64 + q * 16 : 80 + q * 16],
            ],
            0,
        )
        o = dot(rows, hot[...])
        for hh in (0, 1):
            cols = slice(hh * 512, hh * 512 + 512)
            ap[hh, q * 16 : q * 16 + 16] = o[0:16, cols].astype(BF)
            ap[hh, 64 + q * 16 : 80 + q * 16] = o[16:32, cols].astype(BF)
        bl[0, q * 16 : q * 16 + 16] = o[32:48].astype(BF)
        bl[0, 64 + q * 16 : 80 + q * 16] = o[48:64].astype(BF)
        bl[1, q * 16 : q * 16 + 16] = (-o[48:64]).astype(BF)
        bl[1, 64 + q * 16 : 80 + q * 16] = o[32:48].astype(BF)

    permute(0)
    permute(1)
    round_z(5, 6, (6, (0,), 7), (6, (1,), 7))
    side_step(3)
    side_step(4)
    permute(2)
    permute(3)
    for cc in (0, 1):
        z_recv(7, cc)
    x_send(7)
    side_step(5)
    side_step(6)
    transform(2)
    transform(3)
    side_step(7)

    row_q = lax.broadcasted_iota(jnp.int32, (64, 128), 0) // 16
    lane = lax.broadcasted_iota(jnp.int32, (64, 128), 1)
    keep = row_q == (lane % 64) // 16
    flip = jnp.where(lane < 64, F32(1.0), F32(-1.0))

    def fold(d):
        r = d[:64] + flip * pltpu.roll(d[64:], 64, 1)
        r = jnp.where(keep, r, F32(0.0))
        return (r[0:16] + r[16:32]) + (r[32:48] + r[48:64])

    zb[...] = (dens[3].astype(F32) * coulomb[...]).astype(BF)
    res[0, 1] = fold(dot_nt(dens[2], zb[...]))

    def product(hh):
        wr = w[0, hh].reshape(512, 1024)
        wi = w[1, hh].reshape(512, 1024)
        yb[...] = (dot_nt(wr, bl[0]) + dot_nt(wi, bl[1])).astype(BF)
        return dot(ap[hh], yb[...])

    d0 = product(h)
    for k in range(8):
        landed(half(1 - h, k, 1 - xl), xsr.at[k])
    res[0, 0] = fold(d0 + product(1 - h))
    out[c] = res[0]
    send(res.at[0], out.at[c], ss.at[3], sr.at[3], sib)
    landed(out.at[1 - c], sr.at[3])
    for cp in started:
        cp.wait_send()


def moved(w, tr):
    p0, p1 = w[:, 0, 0], w[:, 0, 1]
    axes = ("kx", "ky")

    def shift(a, dx, dy):
        pairs = [
            (((i + dx) % 32) * 8 + (k + dy) % 8, i * 8 + k) for i in range(32) for k in range(8)
        ]
        return lax.ppermute(a, axes, pairs)

    def by_x(t):
        return lambda a, b: (shift(b, t, -1), shift(a, t, 0))

    def by_y(t):
        if t % 2 == 0:
            return lambda a, b: (shift(a, -1, t // 2), shift(b, -1, t // 2))
        return lambda a, b: (shift(b, -1, t // 2), shift(a, -1, t // 2 + 1))

    a0, a1 = lax.switch(tr[0, 0], [by_x(t) for t in range(32)], p0, p1)
    b0, b1 = lax.switch(tr[1, 1], [by_y(t) for t in range(16)], p0, p1)
    return jnp.stack([jnp.stack([a0, a1], 1), jnp.stack([b0, b1], 1)])


def local(waves, screened, coulomb, transfers, gmap):
    there = moved(waves, transfers)
    here = waves[:, 0]
    vmem = pl.BlockSpec(memory_space=pltpu.VMEM)
    hbm = pl.BlockSpec(memory_space=pl.ANY)
    dma = pltpu.SemaphoreType.DMA
    out = pl.pallas_call(
        kernel,
        out_shape=jax.ShapeDtypeStruct((2, 2, 16, 128), F32),
        in_specs=[pl.BlockSpec(memory_space=pltpu.SMEM), hbm, hbm, hbm, vmem, vmem, vmem],
        out_specs=vmem,
        scratch_shapes=[
            pltpu.VMEM((2, 2, 8, 2, 32, 1024), BF),
            pltpu.VMEM((2, 2, 2, 8, 1024), BF),
            pltpu.VMEM((2, 2, 2, 8, 1024), BF),
            pltpu.VMEM((4, 256, 1024), BF),
            pltpu.VMEM((4, 128, 1024), BF),
            pltpu.VMEM((1024, 1024), BF),
            pltpu.VMEM((2, 128, 1024), BF),
            pltpu.VMEM((2, 128, 512), BF),
            pltpu.VMEM((512, 128), BF),
            pltpu.VMEM((128, 1024), BF),
            pltpu.VMEM((1, 2, 16, 128), F32),
            dma((3,)), dma((7, 2)), dma((8, 2)), dma((8,)), dma((8,)), dma((8,)), dma((8,)),
            dma((4,)), dma((4,)),
        ],
        compiler_params=pltpu.CompilerParams(
            collective_id=0, has_side_effects=True, vmem_limit_bytes=48 * 1024 * 1024
        ),
    )(transfers, here, there, screened, gmap.reshape(8, 1024), coulomb.reshape(1, 1024), table())
    r = out.reshape(2, 2, 16, 2, 2, 2, 16)
    c = lax.axis_index("kx") % 2
    mine = jnp.arange(2).reshape(2, 1, 1, 1, 1, 1) == c
    r = jnp.where(mine, r[:, :, :, :, 0], r[:, :, :, :, 1])
    direct = r[:, 0].reshape(2, 4, 4, 2, 2, 4, 4).transpose(0, 3, 4, 5, 1, 6, 2)
    exch = r[:, 1].transpose(0, 2, 3, 1, 4)
    return direct.reshape(2, 2, 1, 2, 256), exch.reshape(2, 2, 1, 2, 256)


def solution(mesh):
    return jax.shard_map(
        local,
        mesh=mesh,
        in_specs=(P(None, "kx", "ky", None, None), P(None, None, "kx", None), P(), P(), P()),
        out_specs=(P(None, None, "kx", "ky", None), P(None, None, "kx", "ky", None)),
        check_vma=False,
    )
```

```python
import functools

import jax
import jax.numpy as jnp
import numpy as np
from jax import lax
from jax.experimental import pallas as pl
from jax.experimental.pallas import tpu as pltpu
from jax.sharding import PartitionSpec as P

MESH = pl.DeviceIdType.MESH
OFFS = (0, -1, 1, -2, 2, -3, 3, 4)
BF = jnp.bfloat16
F32 = jnp.float32
NT = (((1,), (1,)), ((), ()))


def table():
    r = np.arange(1024)
    turns = (r[:, None] * r[None, :512]) % 1024
    angles = turns.astype(np.float32) * np.float32(2.0 * np.pi / 1024)
    both = np.concatenate([np.cos(angles), np.sin(angles)], 1)
    return jnp.asarray(both, dtype=BF)


def dot(a, b):
    return lax.dot_general(a, b, (((1,), (0,)), ((), ())), preferred_element_type=F32)


def dot_nt(a, b):
    return lax.dot_general(a, b, NT, preferred_element_type=F32)


def kernel(
    transfers, waves, scr, gmap, coulomb, tab_hbm, out,
    w, hb, tb, lhs, dens, hot, bl, ap, yb, zb, res,
    tab, gm, cl, eg, fg, xa, xb, tr,
    sem_loc, zs, zr, xds, xdr, xss, xsr, ss, sr,
    es, er, eas, ear, fs, fr, fas, far, x2s, x2r,
):
    kx = lax.axis_index("kx")
    ky = lax.axis_index("ky")
    c = kx % 2
    m = kx // 2
    h = m // 8
    z = m % 8
    y = ky // 2
    xl = ky % 2

    def dev(h_, z_, c_, y_, xl_):
        return ((h_ * 8 + z_) * 2 + c_, y_ * 2 + xl_)

    def at_m(m_, c_):
        return (m_ * 2 + c_, ky)

    up = dev(h, (z + 1) % 8, c, y, xl)
    down = dev(h, (z + 7) % 8, c, y, xl)
    cross = dev(1 - h, z, c, y, 1 - xl)
    side = dev(h, z, c, y, 1 - xl)
    sib = dev(h, z, 1 - c, y, xl)
    over = dev(1 - h, z, c, y, xl)
    y_up = dev(h, z, c, (y + 1) % 4, xl)
    y_down = dev(h, z, c, (y + 3) % 4, xl)
    ky_next, ky_prev = (ky + 1) % 8, (ky + 7) % 8
    m_next, m_prev = (m + 1) % 16, (m + 15) % 16
    ahead, behind = at_m(m_next, 1), at_m(m_prev, 1)
    first = c == 0
    second = c == 1

    own_w = pltpu.make_async_copy(scr.at[c], w.at[:, h, z, c], sem_loc.at[0])
    own_w.start()
    own_h = pltpu.make_async_copy(waves.at[:, 0], hb.at[c], sem_loc.at[1])
    own_h.start()
    get_tab = pltpu.make_async_copy(tab_hbm, tab, sem_loc.at[2])
    get_tab.start()
    get_gm = pltpu.make_async_copy(gmap, gm, sem_loc.at[3])
    get_gm.start()
    get_cl = pltpu.make_async_copy(coulomb, cl, sem_loc.at[4])
    get_cl.start()
    get_tr = pltpu.make_async_copy(transfers, tr, sem_loc.at[6])
    get_tr.start()

    barrier = pltpu.get_barrier_semaphore()

    def greet(d):
        pl.semaphore_signal(barrier, inc=1, device_id=d, device_id_type=MESH)

    for d in (up, down, cross, side, sib, (m * 2, ky_next)):
        greet(d)

    @pl.when(first)
    def _():
        for d in ((m * 2, ky_prev), (m * 2 + 1, ky_prev), over):
            greet(d)
        pl.semaphore_wait(barrier, 9)

    @pl.when(second)
    def _():
        for d in (ahead, behind, y_up, y_down):
            greet(d)
        pl.semaphore_wait(barrier, 10)

    ends = {None: [], 0: [], 1: []}

    def send(src, dst, s, r, d, who=None):
        def make():
            return pltpu.make_async_remote_copy(
                src_ref=src(), dst_ref=dst(), send_sem=s(), recv_sem=r(), device_id=d, device_id_type=MESH
            )

        make().start()
        ends[who].append(make)

    def landed(dst, r):
        pltpu.make_async_remote_copy(
            src_ref=dst, dst_ref=dst, send_sem=ss.at[0], recv_sem=r, device_id=sib, device_id_type=MESH
        ).wait_recv()

    def zb_of(k):
        return (z + OFFS[k] + 8) % 8

    def half(hh, k, cc):
        return w.at[:, hh, zb_of(k), cc]

    send(lambda: waves.at[:, 0, 1], lambda: eg.at[z, c, :, 0], lambda: eas.at[0], lambda: ear.at[c, 0], (m * 2, ky_next))

    @pl.when(first)
    def _():
        pltpu.make_async_copy(waves.at[:, 0, 0], eg.at[z, 0, :, 1], sem_loc.at[5]).start()
        send(lambda: waves.at[:, 0], lambda: fg.at[y, 1], lambda: fas.at[0], lambda: far.at[1], sib, 0)

    @pl.when(second)
    def _():
        send(lambda: waves.at[:, 0, 0], lambda: eg.at[z, 1, :, 1], lambda: eas.at[1], lambda: ear.at[1, 1], sib, 1)
        send(lambda: waves.at[:, 0], lambda: fg.at[y, 0], lambda: fas.at[0], lambda: far.at[0], ahead, 1)

    send(lambda: waves.at[:, 0], lambda: hb.at[c], lambda: ss.at[0], lambda: sr.at[0], sib)
    send(lambda: scr.at[1 - c], lambda: w.at[:, h, z, c], lambda: ss.at[2], lambda: sr.at[2], sib)

    def z_send(k, cc, n, d, k2):
        send(lambda: half(h, k, cc), lambda: half(h, k, cc), lambda: zs.at[n, cc], lambda: zr.at[k2, cc], d)

    def x_send(k):
        cc = 1 - xl
        send(lambda: half(h, k, cc), lambda: half(h, k, cc), lambda: xds.at[k], lambda: xdr.at[k], cross)

    def z_recv(k, cc):
        landed(half(h, k, cc), zr.at[k, cc])

    def side_step(k):
        landed(half(1 - h, k, xl), xdr.at[k])
        send(lambda: half(1 - h, k, xl), lambda: half(1 - h, k, xl), lambda: xss.at[k], lambda: xsr.at[k], side)

    def e_send(k, p, n, d, k2):
        send(lambda: eg.at[zb_of(k), p], lambda: eg.at[zb_of(k), p], lambda: es.at[n, p], lambda: er.at[k2, p], d, 0)

    def e_recv(k, p):
        landed(eg.at[zb_of(k), p], er.at[k, p])

    def yb_of(k):
        return (y + (0, 3, 1, 2)[k]) % 4

    def f_send(k, p, n, d, k2):
        send(lambda: fg.at[yb_of(k), p], lambda: fg.at[yb_of(k), p], lambda: fs.at[n, p], lambda: fr.at[k2, p], d, 1)

    def f_recv(k, p):
        landed(fg.at[yb_of(k), p], fr.at[k, p])

    @pl.when(first)
    def _():
        landed(eg.at[z, 0, :, 0], ear.at[0, 0])
        landed(eg.at[z, 1, :, 0], ear.at[1, 0])
        landed(eg.at[z, 1, :, 1], ear.at[1, 1])
        pltpu.make_async_copy(waves.at[:, 0, 0], eg.at[z, 0, :, 1], sem_loc.at[5]).wait()
        for p in (0, 1):
            e_send(0, p, 0, up, 1)
            e_send(0, p, 1, down, 2)

    @pl.when(second)
    def _():
        for p in (1, 0):
            landed(fg.at[y, p], far.at[p])
            f_send(0, p, 0, y_up, 1)
            f_send(0, p, 1, y_down, 2)

    own_w.wait()
    landed(w.at[:, h, z, 1 - c], sr.at[2])
    for cc in (0, 1):
        z_send(0, cc, 0, up, 1)
        z_send(0, cc, 1, down, 2)
    x_send(0)

    low = lax.broadcasted_iota(jnp.int32, (8, 1024), 0) < 4
    odd = lax.broadcasted_iota(jnp.int32, (8, 1024), 1) % 2 == 1
    sign = jnp.where(odd, F32(-1.0), F32(1.0))
    sign = jnp.concatenate([sign, sign], 0)

    def left(x, at):
        rows = [jnp.broadcast_to(x[at + i : at + i + 1], (8, 1024)) for i in range(4)]
        return jnp.where(low, rows[0], rows[1]), jnp.where(low, rows[2], rows[3])

    def right(x):
        sw = pltpu.roll(x, 4, 0)
        return jnp.where(low, x, sw), jnp.where(low, sw, x)

    def pair(t, q, lr, li, rr, ri):
        re = jnp.concatenate([lr[i] * rr + li[i] * ri for i in (0, 1)], 0)
        im = jnp.concatenate([lr[i] * ri - li[i] * rr for i in (0, 1)], 0)
        lhs[t, q * 16 : q * 16 + 16] = re.astype(BF)
        lhs[t, 64 + q * 16 : 80 + q * 16] = im.astype(BF)
        lhs[t, 128 + q * 16 : 144 + q * 16] = (re * sign).astype(BF)
        lhs[t, 192 + q * 16 : 208 + q * 16] = (im * sign).astype(BF)

    def round_half(ka, kb, na, nb, cc):
        z_recv(ka, cc)
        if na is not None and (na[1] is None or cc in na[1]):
            z_send(ka, cc, na[0], up, na[2])
        z_recv(kb, cc)
        if nb is not None and (nb[1] is None or cc in nb[1]):
            z_send(kb, cc, nb[0], down, nb[2])

    def round_x(ka, kb):
        x_send(ka)
        x_send(kb)

    def transform(t):
        for g in (0, 1):
            o = dot(lhs[t, g * 128 : g * 128 + 128], tab[...])
            cols = slice(512, 1024) if g == 0 else slice(0, 512)
            dens[t, :64, cols] = (o[:64, :512] + o[64:, 512:]).astype(BF)
            dens[t, 64:, cols] = (o[64:, :512] - o[:64, 512:]).astype(BF)

    own_h.wait()
    landed(hb.at[1 - c], sr.at[0])
    for q in range(4):
        hre = hb[q // 2, 0, q % 2].astype(F32)
        him = hb[q // 2, 1, q % 2].astype(F32)
        pair(2, q, left(hre, 0), left(him, 0), right(hre)[1], right(him)[1])
    get_tab.wait()

    @pl.when(first)
    def _():
        for p in (0, 1):
            e_recv(1, p)
            e_send(1, p, 2, up, 3)
            e_recv(2, p)
            e_send(2, p, 3, down, 4)

    @pl.when(second)
    def _():
        f_recv(1, 0)
        f_send(1, 0, 2, y_up, 3)
        f_recv(2, 1)
        f_send(2, 1, 2, y_down, 3)

    round_half(1, 2, (2, None, 3), (3, None, 4), 0)
    transform(2)

    @pl.when(first)
    def _():
        for p in (0, 1):
            e_recv(3, p)
            if p == 0:
                e_send(3, p, 4, up, 5)
            else:
                e_send(3, p, 4, up, 5)
            e_recv(4, p)
            e_send(4, p, 5, down, 6)

    round_half(1, 2, (2, None, 3), (3, None, 4), 1)
    round_x(1, 2)
    side_step(0)

    get_tr.wait()
    get_gm.wait()

    @pl.when(first)
    def _():
        for p in (0, 1):
            e_recv(5, p)
            if p == 0:
                e_send(5, p, 6, up, 7)
            e_recv(6, p)
            if p == 1:
                e_send(6, p, 6, down, 7)

    def spots_y(own_ky):
        got = []
        for pt in (0, 1):
            g = own_ky * 2 + pt + tr[1, 1]
            ky_t = (g // 2) % 8
            got.append((ky_t // 2, ky_t % 2, g % 2))
        return got

    def spots_x():
        got = []
        for p in (0, 1):
            k_t = (m * 2 + p + tr[0, 0]) % 32
            got.append((k_t // 16, (k_t // 2) % 8, k_t % 2))
        return got

    @pl.when(second)
    def _():
        f_recv(1, 1)
        f_recv(2, 0)
        f_recv(3, 0)
        f_recv(3, 1)
        for pt, (y_t, _, p_t) in enumerate(spots_y(y * 2 + 1 - xl)):
            for p in (0, 1):
                for ri in (0, 1):
                    xa[pt, p, ri] = fg[y_t, p, ri, p_t]
        send(lambda: xa, lambda: xb, lambda: x2s.at[0], lambda: x2r.at[0], side, 1)

    round_half(3, 4, (4, None, 5), (5, None, 6), 0)

    @pl.when(first)
    def _():
        for p in (0, 1):
            e_recv(7, p)
        for p, (_, z_t, p_t) in enumerate(spots_x()):
            for ri in (0, 1):
                for pt in (0, 1):
                    xa[p, ri, pt] = eg[z_t, p_t, ri, pt]
        send(lambda: xa, lambda: xb, lambda: x2s.at[0], lambda: x2r.at[0], over, 0)

    round_half(3, 4, (4, None, 5), (5, None, 6), 1)
    round_x(3, 4)
    side_step(1)
    side_step(2)

    zero = lax.broadcasted_iota(jnp.int32, (8, 1024), 0) * 0

    @pl.when(first)
    def _():
        landed(xb, x2r.at[0])
        for p, (h_t, z_t, p_t) in enumerate(spots_x()):
            near = zero + h_t == h
            for ri in (0, 1):
                for pt in (0, 1):
                    tb[p, ri, pt] = jnp.where(
                        near, eg[z_t, p_t, ri, pt].astype(F32), xb[p, ri, pt].astype(F32)
                    ).astype(BF)

    @pl.when(second)
    def _():
        landed(xb, x2r.at[0])
        for pt, (y_t, xl_t, p_t) in enumerate(spots_y(ky)):
            near = zero + xl_t == xl
            for p in (0, 1):
                for ri in (0, 1):
                    tb[p, ri, pt] = jnp.where(
                        near, fg[y_t, p, ri, p_t].astype(F32), xb[pt, p, ri].astype(F32)
                    ).astype(BF)

    for q in range(4):
        p, pt = q // 2, q % 2
        hre = hb[p, 0, pt].astype(F32)
        him = hb[p, 1, pt].astype(F32)
        tre = tb[p, 0, pt].astype(F32)
        tim = tb[p, 1, pt].astype(F32)
        (trv, trc), (tiv, tic) = right(tre), right(tim)
        pair(0, q, left(hre, 4), left(him, 4), trc, tic)
        pair(1, q, left(hre, 0), left(him, 0), trv, tiv)
        pair(3, q, left(tre, 0), left(tim, 0), trc, tic)

    transform(0)
    round_half(5, 6, (6, (0,), 7), (6, (1,), 7), 0)
    transform(1)
    round_half(5, 6, (6, (0,), 7), (6, (1,), 7), 1)
    round_x(5, 6)
    side_step(3)
    side_step(4)

    def permute(q):
        p, pt = q // 2, q % 2
        wx = jnp.where(m * 2 + p + tr[c, 0] >= 32, 1, 0)
        wy = jnp.where(ky * 2 + pt + tr[c, 1] >= 16, 2, 0)
        row = gm[c, pl.ds(wx + wy, 1), :]
        hot[...] = jnp.where(
            lax.broadcasted_iota(jnp.int32, (1024, 1024), 0) == row, F32(1.0), F32(0.0)
        ).astype(BF)
        rows = jnp.concatenate(
            [
                dens[0, q * 16 : q * 16 + 16],
                dens[0, 64 + q * 16 : 80 + q * 16],
                dens[1, q * 16 : q * 16 + 16],
                dens[1, 64 + q * 16 : 80 + q * 16],
            ],
            0,
        )
        o = dot(rows, hot[...])
        for hh in (0, 1):
            cols = slice(hh * 512, hh * 512 + 512)
            ap[hh, q * 16 : q * 16 + 16] = o[0:16, cols].astype(BF)
            ap[hh, 64 + q * 16 : 80 + q * 16] = o[16:32, cols].astype(BF)
        bl[0, q * 16 : q * 16 + 16] = o[32:48].astype(BF)
        bl[0, 64 + q * 16 : 80 + q * 16] = o[48:64].astype(BF)
        bl[1, q * 16 : q * 16 + 16] = (-o[48:64]).astype(BF)
        bl[1, 64 + q * 16 : 80 + q * 16] = o[32:48].astype(BF)

    permute(0)
    permute(1)
    for cc in (0, 1):
        z_recv(7, cc)
    x_send(7)
    side_step(5)
    side_step(6)
    permute(2)
    permute(3)
    side_step(7)
    transform(3)

    row_q = lax.broadcasted_iota(jnp.int32, (64, 128), 0) // 16
    lane = lax.broadcasted_iota(jnp.int32, (64, 128), 1)
    keep = row_q == (lane % 64) // 16
    flip = jnp.where(lane < 64, F32(1.0), F32(-1.0))

    def fold(d):
        r = d[:64] + flip * pltpu.roll(d[64:], 64, 1)
        r = jnp.where(keep, r, F32(0.0))
        return (r[0:16] + r[16:32]) + (r[32:48] + r[48:64])

    get_cl.wait()
    zb[...] = (dens[3].astype(F32) * cl[...]).astype(BF)
    res[0, 1] = fold(dot_nt(dens[2], zb[...]))

    def product(hh):
        wr = w[0, hh].reshape(512, 1024)
        wi = w[1, hh].reshape(512, 1024)
        yb[...] = (dot_nt(wr, bl[0]) + dot_nt(wi, bl[1])).astype(BF)
        return dot(ap[hh], yb[...])

    d0 = product(h)
    for k in range(8):
        landed(half(1 - h, k, 1 - xl), xsr.at[k])
    res[0, 0] = fold(d0 + product(1 - h))
    out[c] = res[0]
    send(lambda: res.at[0], lambda: out.at[c], lambda: ss.at[3], lambda: sr.at[3], sib)
    landed(out.at[1 - c], sr.at[3])
    for make in ends[None]:
        make().wait_send()

    @pl.when(first)
    def _():
        for make in ends[0]:
            make().wait_send()

    @pl.when(second)
    def _():
        for make in ends[1]:
            make().wait_send()


def local(waves, screened, coulomb, transfers, gmap):
    vmem = pl.BlockSpec(memory_space=pltpu.VMEM)
    hbm = pl.BlockSpec(memory_space=pl.ANY)
    dma = pltpu.SemaphoreType.DMA
    out = pl.pallas_call(
        kernel,
        out_shape=jax.ShapeDtypeStruct((2, 2, 16, 128), F32),
        in_specs=[hbm] * 6,
        out_specs=vmem,
        scratch_shapes=[
            pltpu.VMEM((2, 2, 8, 2, 32, 1024), BF),
            pltpu.VMEM((2, 2, 2, 8, 1024), BF),
            pltpu.VMEM((2, 2, 2, 8, 1024), BF),
            pltpu.VMEM((4, 256, 1024), BF),
            pltpu.VMEM((4, 128, 1024), BF),
            pltpu.VMEM((1024, 1024), BF),
            pltpu.VMEM((2, 128, 1024), BF),
            pltpu.VMEM((2, 128, 512), BF),
            pltpu.VMEM((512, 128), BF),
            pltpu.VMEM((128, 1024), BF),
            pltpu.VMEM((1, 2, 16, 128), F32),
            pltpu.VMEM((1024, 1024), BF),
            pltpu.VMEM((2, 4, 1024), jnp.int32),
            pltpu.VMEM((1024,), F32),
            pltpu.VMEM((8, 2, 2, 2, 8, 1024), BF),
            pltpu.VMEM((4, 2, 2, 2, 8, 1024), BF),
            pltpu.VMEM((2, 2, 2, 8, 1024), BF),
            pltpu.VMEM((2, 2, 2, 8, 1024), BF),
            pltpu.SMEM((2, 2), jnp.int32),
            dma((7,)), dma((7, 2)), dma((8, 2)), dma((8,)), dma((8,)), dma((8,)), dma((8,)),
            dma((4,)), dma((4,)),
            dma((7, 2)), dma((8, 2)), dma((2,)), dma((2, 2)), dma((3, 2)), dma((4, 2)), dma((1,)), dma((2,)),
            dma((1,)), dma((1,)),
        ],
        compiler_params=pltpu.CompilerParams(
            collective_id=0, has_side_effects=True, vmem_limit_bytes=60 * 1024 * 1024
        ),
    )(transfers, waves, screened, gmap, coulomb, table())
    r = out.reshape(2, 2, 16, 2, 2, 2, 16)
    first = lax.axis_index("kx") % 2 == 0
    r = jnp.where(first, r[:, :, :, :, 0], r[:, :, :, :, 1])
    direct = r[:, 0].reshape(2, 4, 4, 2, 2, 4, 4).transpose(0, 3, 4, 5, 1, 6, 2)
    exch = r[:, 1].transpose(0, 2, 3, 1, 4)
    return direct.reshape(2, 2, 1, 2, 256), exch.reshape(2, 2, 1, 2, 256)


def solution(mesh):
    return jax.shard_map(
        local,
        mesh=mesh,
        in_specs=(P(None, "kx", "ky", None, None), P(None, None, "kx", None), P(), P(), P()),
        out_specs=(P(None, None, "kx", "ky", None), P(None, None, "kx", "ky", None)),
        check_vma=False,
    )
```

```python
import functools

import jax
import jax.numpy as jnp
import numpy as np
from jax import lax
from jax.experimental import pallas as pl
from jax.experimental.pallas import tpu as pltpu
from jax.sharding import PartitionSpec as P

MESH = pl.DeviceIdType.MESH
OFFS = (0, -1, 1, -2, 2, -3, 3, 4)
BF = jnp.bfloat16
F32 = jnp.float32
NT = (((1,), (1,)), ((), ()))


def table():
    r = np.arange(1024)
    turns = (r[:, None] * r[None, :512]) % 1024
    angles = turns.astype(np.float32) * np.float32(2.0 * np.pi / 1024)
    both = np.concatenate([np.cos(angles), np.sin(angles)], 1)
    return jnp.asarray(both, dtype=BF)


def dot(a, b):
    return lax.dot_general(a, b, (((1,), (0,)), ((), ())), preferred_element_type=F32)


def dot_nt(a, b):
    return lax.dot_general(a, b, NT, preferred_element_type=F32)


def kernel(
    transfers, waves, scr, gmap, coulomb, tab_hbm, out,
    w, hb, tb, lhs, dens, hot, bl, ap, blp, app, yb, zb, res, part,
    tab, gm, cl, eg, fg, xa, xb, tr,
    sem_loc, zs, zr, ys, yr, ss, sr,
    es, er, eas, ear, fs, fr, fas, far, x2s, x2r, bs, br, ps, pr,
):
    kx = lax.axis_index("kx")
    ky = lax.axis_index("ky")
    c = kx % 2
    m = kx // 2
    h = m // 8
    z = m % 8
    y = ky // 2
    xl = ky % 2
    e = y % 2

    def dev(h_, z_, c_, ky_):
        return ((h_ * 8 + z_) * 2 + c_, ky_)

    ky_next, ky_prev = (ky + 1) % 8, (ky + 7) % 8
    m_next, m_prev = (m + 1) % 16, (m + 15) % 16
    other_ky = y * 2 + 1 - xl
    up = dev(h, (z + 1) % 8, c, ky)
    down = dev(h, (z + 7) % 8, c, ky)
    cross = dev(1 - h, z, c, other_ky)
    diag = dev(1 - h, z, 1 - c, other_ky)
    side = dev(h, z, c, other_ky)
    sib = dev(h, z, 1 - c, ky)
    over = dev(1 - h, z, c, ky)
    y_up = dev(h, z, c, (ky + 2) % 8)
    y_down = dev(h, z, c, (ky + 6) % 8)
    next_near, next_far = dev(h, z, c, ky_next), dev(1 - h, z, c, ky_next)
    prev_near, prev_far = dev(h, z, c, ky_prev), dev(1 - h, z, c, ky_prev)
    ahead, behind = (m_next * 2 + 1, ky), (m_prev * 2 + 1, ky)
    last = (jnp.where(c == 0, up[0], down[0]), ky)
    last_y = (kx, jnp.where(c == 0, y_up[1], y_down[1]))
    first = c == 0
    second = c == 1

    own_w = pltpu.make_async_copy(scr.at[c], w.at[:, z, c], sem_loc.at[0])
    own_w.start()
    own_h = pltpu.make_async_copy(waves.at[:, 0], hb.at[c], sem_loc.at[1])
    own_h.start()
    get_tab = pltpu.make_async_copy(tab_hbm, tab, sem_loc.at[2])
    get_tab.start()
    get_gm = pltpu.make_async_copy(gmap, gm, sem_loc.at[3])
    get_gm.start()
    get_cl = pltpu.make_async_copy(coulomb, cl, sem_loc.at[4])
    get_cl.start()
    get_tr = pltpu.make_async_copy(transfers, tr, sem_loc.at[6])
    get_tr.start()

    barrier = pltpu.get_barrier_semaphore()

    def greet(d):
        pl.semaphore_signal(barrier, inc=1, device_id=d, device_id_type=MESH)

    for d in (up, down, cross, diag, sib, y_up, y_down):
        greet(d)

    @pl.when(first)
    def _():
        for d in (over, next_near, next_far, prev_near, prev_far):
            greet(d)
        pl.semaphore_wait(barrier, 12)

    @pl.when(second)
    def _():
        for d in (side, ahead, behind):
            greet(d)
        pl.semaphore_wait(barrier, 10)

    ends = {None: [], 0: [], 1: []}

    def send(src, dst, s, r, d, who=None):
        def make():
            return pltpu.make_async_remote_copy(
                src_ref=src(), dst_ref=dst(), send_sem=s(), recv_sem=r(), device_id=d, device_id_type=MESH
            )

        make().start()
        ends[who].append(make)

    def landed(dst, r):
        pltpu.make_async_remote_copy(
            src_ref=dst, dst_ref=dst, send_sem=ss.at[0], recv_sem=r, device_id=sib, device_id_type=MESH
        ).wait_recv()

    def zb_of(k):
        return (z + OFFS[k] + 8) % 8

    def yb_of(k):
        return (y + (0, 3, 1, 2)[k]) % 4

    def e_send(k, p, n, d, k2):
        send(lambda: eg.at[zb_of(k), p], lambda: eg.at[zb_of(k), p], lambda: es.at[n, p], lambda: er.at[k2, p], d, 0)

    def e_recv(k, p):
        landed(eg.at[zb_of(k), p], er.at[k, p])

    def f_send(k, p, n, d, k2):
        send(lambda: fg.at[yb_of(k), p], lambda: fg.at[yb_of(k), p], lambda: fs.at[n, p], lambda: fr.at[k2, p], d, 1)

    def f_recv(k, p):
        landed(fg.at[yb_of(k), p], fr.at[k, p])

    @pl.when(first)
    def _():
        send(lambda: waves.at[:, 0], lambda: eg.at[z, 0], lambda: es.at[0, 0], lambda: er.at[1, 0], up, 0)
        send(lambda: waves.at[:, 0], lambda: eg.at[z, 0], lambda: es.at[1, 0], lambda: er.at[2, 0], down, 0)
        pltpu.make_async_copy(waves.at[:, 0], eg.at[z, 0], sem_loc.at[5]).start()
        send(lambda: waves.at[:, 0], lambda: fg.at[y, 1], lambda: fas.at[0], lambda: far.at[1], sib, 0)

    @pl.when(second)
    def _():
        send(lambda: waves.at[:, 0], lambda: eg.at[z, 1], lambda: eas.at[0], lambda: ear.at[0], sib, 1)
        send(lambda: waves.at[:, 0], lambda: fg.at[y, 0], lambda: fas.at[0], lambda: far.at[0], ahead, 1)

    send(lambda: scr.at[1 - c], lambda: w.at[:, z, c], lambda: ss.at[2], lambda: sr.at[2], sib)
    send(lambda: waves.at[:, 0], lambda: hb.at[c], lambda: ss.at[0], lambda: sr.at[0], sib)

    @pl.when(first)
    def _():
        landed(eg.at[z, 1], ear.at[0])
        e_send(0, 1, 0, up, 1)
        e_send(0, 1, 1, down, 2)

    @pl.when(second)
    def _():
        for p in (1, 0):
            landed(fg.at[y, p], far.at[p])
            f_send(0, p, 0, y_up, 1)
            f_send(0, p, 1, y_down, 2)

    def block(k, cc):
        return w.at[:, zb_of(k), cc]

    def w_send(k, n, d, k2):
        send(lambda: block(k, e), lambda: block(k, e), lambda: zs.at[n], lambda: zr.at[k2], d)

    def w_recv(k):
        landed(block(k, e), zr.at[k])
        d = last_y if k == 7 else (y_up if k % 2 == 1 else y_down)
        send(lambda: block(k, e), lambda: block(k, e), lambda: ys.at[k], lambda: yr.at[k], d)

    own_w.wait()
    landed(w.at[:, z, 1 - c], sr.at[2])
    w_send(0, 0, up, 1)
    w_send(0, 1, down, 2)

    low = lax.broadcasted_iota(jnp.int32, (8, 1024), 0) < 4
    odd = lax.broadcasted_iota(jnp.int32, (8, 1024), 1) % 2 == 1
    sign = jnp.where(odd, F32(-1.0), F32(1.0))
    sign = jnp.concatenate([sign, sign], 0)

    def left(x, at):
        rows = [jnp.broadcast_to(x[at + i : at + i + 1], (8, 1024)) for i in range(4)]
        return jnp.where(low, rows[0], rows[1]), jnp.where(low, rows[2], rows[3])

    def right(x):
        sw = pltpu.roll(x, 4, 0)
        return jnp.where(low, x, sw), jnp.where(low, sw, x)

    def pair(t, q, lr, li, rr, ri):
        re = jnp.concatenate([lr[i] * rr + li[i] * ri for i in (0, 1)], 0)
        im = jnp.concatenate([lr[i] * ri - li[i] * rr for i in (0, 1)], 0)
        lhs[t, q * 16 : q * 16 + 16] = re.astype(BF)
        lhs[t, 64 + q * 16 : 80 + q * 16] = im.astype(BF)
        lhs[t, 128 + q * 16 : 144 + q * 16] = (re * sign).astype(BF)
        lhs[t, 192 + q * 16 : 208 + q * 16] = (im * sign).astype(BF)

    def transform(t):
        for g in (0, 1):
            o = dot(lhs[t, g * 128 : g * 128 + 128], tab[...])
            cols = slice(512, 1024) if g == 0 else slice(0, 512)
            dens[t, :64, cols] = (o[:64, :512] + o[64:, 512:]).astype(BF)
            dens[t, 64:, cols] = (o[64:, :512] - o[:64, 512:]).astype(BF)

    @pl.when(first)
    def _():
        for p in (0, 1):
            e_recv(1, p)
            e_send(1, p, 2, up, 3)
            e_recv(2, p)
            e_send(2, p, 3, down, 4)

    @pl.when(second)
    def _():
        f_recv(1, 0)
        f_send(1, 0, 2, y_up, 3)
        f_recv(2, 1)
        f_send(2, 1, 2, y_down, 3)

    own_h.wait()
    landed(hb.at[1 - c], sr.at[0])
    for q in range(4):
        hre = hb[q // 2, 0, q % 2].astype(F32)
        him = hb[q // 2, 1, q % 2].astype(F32)
        pair(2, q, left(hre, 0), left(him, 0), right(hre)[1], right(him)[1])
    get_tab.wait()
    get_tr.wait()
    get_gm.wait()

    def spots_y(own_ky):
        got = []
        for pt in (0, 1):
            g = own_ky * 2 + pt + tr[1, 1]
            ky_t = (g // 2) % 8
            got.append((ky_t // 2, ky_t % 2, g % 2))
        return got

    def spots_x():
        got = []
        for p in (0, 1):
            k_t = (m * 2 + p + tr[0, 0]) % 32
            got.append((k_t // 16, (k_t // 2) % 8, k_t % 2))
        return got

    @pl.when(first)
    def _():
        for p in (0, 1):
            e_recv(3, p)
            e_send(3, p, 4, up, 5)
            e_recv(4, p)
            e_send(4, p, 5, down, 6)

    @pl.when(second)
    def _():
        f_recv(1, 1)
        f_recv(2, 0)
        f_recv(3, 0)
        f_recv(3, 1)
        for pt, (y_t, _, p_t) in enumerate(spots_y(other_ky)):
            for p in (0, 1):
                for ri in (0, 1):
                    xa[pt, p, ri] = fg[y_t, p, ri, p_t]
        send(lambda: xa, lambda: xb.at[0], lambda: x2s.at[0], lambda: x2r.at[0], side, 1)

    w_recv(1)
    w_send(1, 2, up, 3)
    w_recv(2)
    w_send(2, 3, down, 4)
    transform(2)

    @pl.when(first)
    def _():
        for p in (0, 1):
            e_recv(5, p)
            if p == 0:
                e_send(5, p, 6, up, 7)
            e_recv(6, p)
            if p == 1:
                e_send(6, p, 6, down, 7)

    w_recv(3)
    w_send(3, 4, up, 5)
    w_recv(4)
    w_send(4, 5, down, 6)

    @pl.when(first)
    def _():
        pltpu.make_async_copy(waves.at[:, 0], eg.at[z, 0], sem_loc.at[5]).wait()
        for p in (0, 1):
            e_recv(7, p)
        for p, (_, z_t, p_t) in enumerate(spots_x()):
            for ri in (0, 1):
                for pt in (0, 1):
                    xa[pt, p, ri] = eg[z_t, p_t, ri, pt]
        send(lambda: xa.at[1], lambda: xb.at[1, 0], lambda: x2s.at[1], lambda: x2r.at[1], next_near, 0)
        send(lambda: xa.at[1], lambda: xb.at[1, 1], lambda: x2s.at[2], lambda: x2r.at[2], next_far, 0)
        send(lambda: xa.at[0], lambda: xb.at[0, 0], lambda: x2s.at[0], lambda: x2r.at[0], over, 0)

    w_recv(5)
    w_recv(6)
    k_last = jnp.where(c == 0, (z + 5) % 8, (z + 3) % 8)
    send(lambda: w.at[:, k_last, e], lambda: w.at[:, k_last, e], lambda: zs.at[6], lambda: zr.at[7], last)

    zero = lax.broadcasted_iota(jnp.int32, (8, 1024), 0) * 0

    @pl.when(first)
    def _():
        landed(xb.at[0, 0], x2r.at[0])
        landed(xb.at[1, 0], x2r.at[1])
        landed(xb.at[1, 1], x2r.at[2])
        for p, (h_t, _, _) in enumerate(spots_x()):
            near = zero + h_t == h
            for ri in (0, 1):
                tb[p, ri, 1] = jnp.where(near, xa[0, p, ri].astype(F32), xb[0, 0, p, ri].astype(F32)).astype(BF)
                tb[p, ri, 0] = jnp.where(near, xb[1, 0, p, ri].astype(F32), xb[1, 1, p, ri].astype(F32)).astype(BF)

    @pl.when(second)
    def _():
        landed(xb.at[0], x2r.at[0])
        for pt, (y_t, xl_t, p_t) in enumerate(spots_y(ky)):
            near = zero + xl_t == xl
            for p in (0, 1):
                for ri in (0, 1):
                    tb[p, ri, pt] = jnp.where(
                        near, fg[y_t, p, ri, p_t].astype(F32), xb[0, pt, p, ri].astype(F32)
                    ).astype(BF)

    for q in range(4):
        p, pt = q // 2, q % 2
        hre = hb[p, 0, pt].astype(F32)
        him = hb[p, 1, pt].astype(F32)
        tre = tb[p, 0, pt].astype(F32)
        tim = tb[p, 1, pt].astype(F32)
        (trv, trc), (tiv, tic) = right(tre), right(tim)
        pair(0, q, left(hre, 4), left(him, 4), trc, tic)
        pair(1, q, left(hre, 0), left(him, 0), trv, tiv)
        pair(3, q, left(tre, 0), left(tim, 0), trc, tic)

    transform(0)
    transform(1)

    def permute(q):
        p, pt = q // 2, q % 2
        wx = jnp.where(m * 2 + p + tr[c, 0] >= 32, 1, 0)
        wy = jnp.where(ky * 2 + pt + tr[c, 1] >= 16, 2, 0)
        row = gm[c, pl.ds(wx + wy, 1), :]
        hot[...] = jnp.where(
            lax.broadcasted_iota(jnp.int32, (1024, 1024), 0) == row, F32(1.0), F32(0.0)
        ).astype(BF)
        at = slice(q * 16, q * 16 + 16)
        rows = jnp.concatenate(
            [dens[0, at], dens[0, 64 + q * 16 : 80 + q * 16], dens[1, at], dens[1, 64 + q * 16 : 80 + q * 16]], 0
        )
        o = dot(rows, hot[...]).astype(BF)
        for hh in (0, 1):
            cols = slice(hh * 512, hh * 512 + 512)
            ap[hh, 0, at] = o[0:16, cols]
            ap[hh, 1, at] = o[16:32, cols]
        bl[0, 0, at] = o[32:48]
        bl[0, 1, at] = o[48:64]
        bl[1, 0, at] = -o[48:64]
        bl[1, 1, at] = o[32:48]

    def share(p):
        at = pl.ds(p * 32, 32)
        send(lambda: bl.at[0, :, at], lambda: blp.at[0, :, at], lambda: bs.at[p, 0], lambda: br.at[p, 0], cross)
        send(lambda: ap.at[1 - h, :, at], lambda: app.at[:, at], lambda: bs.at[p, 1], lambda: br.at[p, 1], cross)

    permute(0)
    permute(1)
    share(0)
    w_recv(7)
    permute(2)
    permute(3)
    share(1)

    row_q = lax.broadcasted_iota(jnp.int32, (64, 128), 0) // 16
    lane = lax.broadcasted_iota(jnp.int32, (64, 128), 1)
    keep = row_q == (lane % 64) // 16
    flip = jnp.where(lane < 64, F32(1.0), F32(-1.0))

    def fold(d):
        r = d[:64] + flip * pltpu.roll(d[64:], 64, 1)
        r = jnp.where(keep, r, F32(0.0))
        return (r[0:16] + r[16:32]) + (r[32:48] + r[48:64])

    transform(3)
    get_cl.wait()
    zb[...] = (dens[3].astype(F32) * cl[...]).astype(BF)
    res[1] = fold(dot_nt(dens[2], zb[...]))

    for k in range(1, 8):
        landed(block(k, 1 - e), yr.at[k])

    def product(b, a):
        wr = w[0].reshape(512, 1024)
        wi = w[1].reshape(512, 1024)
        yb[...] = (dot_nt(wr, b[0].reshape(128, 1024)) + dot_nt(wi, b[1].reshape(128, 1024))).astype(BF)
        return fold(dot(a.reshape(128, 512), yb[...]))

    res[0] = product(bl, ap[h])
    for p in (0, 1):
        at = pl.ds(p * 32, 32)
        landed(blp.at[0, :, at], br.at[p, 0])
        landed(app.at[:, at], br.at[p, 1])
    blp[1, 0] = -blp[0, 1]
    blp[1, 1] = blp[0, 0]
    send(lambda: res, lambda: part.at[0], lambda: ps.at[0], lambda: pr.at[0], sib)
    res_far = product(blp, app[...])
    part[3, 0] = res_far
    send(lambda: part.at[3, 0], lambda: part.at[1, 0], lambda: ps.at[1], lambda: pr.at[1], cross)
    send(lambda: part.at[3, 0], lambda: part.at[2, 0], lambda: ps.at[2], lambda: pr.at[2], diag)
    landed(part.at[0], pr.at[0])
    landed(part.at[1, 0], pr.at[1])
    landed(part.at[2, 0], pr.at[2])
    out[c, 0] = res[0] + part[1, 0]
    out[c, 1] = res[1]
    out[1 - c, 0] = part[0, 0] + part[2, 0]
    out[1 - c, 1] = part[0, 1]
    for make in ends[None]:
        make().wait_send()

    @pl.when(first)
    def _():
        for make in ends[0]:
            make().wait_send()

    @pl.when(second)
    def _():
        for make in ends[1]:
            make().wait_send()


def local(waves, screened, coulomb, transfers, gmap):
    vmem = pl.BlockSpec(memory_space=pltpu.VMEM)
    hbm = pl.BlockSpec(memory_space=pl.ANY)
    dma = pltpu.SemaphoreType.DMA
    out = pl.pallas_call(
        kernel,
        out_shape=jax.ShapeDtypeStruct((2, 2, 16, 128), F32),
        in_specs=[hbm] * 6,
        out_specs=vmem,
        scratch_shapes=[
            pltpu.VMEM((2, 8, 2, 32, 1024), BF),
            pltpu.VMEM((2, 2, 2, 8, 1024), BF),
            pltpu.VMEM((2, 2, 2, 8, 1024), BF),
            pltpu.VMEM((4, 256, 1024), BF),
            pltpu.VMEM((4, 128, 1024), BF),
            pltpu.VMEM((1024, 1024), BF),
            pltpu.VMEM((2, 2, 64, 1024), BF),
            pltpu.VMEM((2, 2, 64, 512), BF),
            pltpu.VMEM((2, 2, 64, 1024), BF),
            pltpu.VMEM((2, 64, 512), BF),
            pltpu.VMEM((512, 128), BF),
            pltpu.VMEM((128, 1024), BF),
            pltpu.VMEM((2, 16, 128), F32),
            pltpu.VMEM((4, 2, 16, 128), F32),
            pltpu.VMEM((1024, 1024), BF),
            pltpu.VMEM((2, 4, 1024), jnp.int32),
            pltpu.VMEM((1024,), F32),
            pltpu.VMEM((8, 2, 2, 2, 8, 1024), BF),
            pltpu.VMEM((4, 2, 2, 2, 8, 1024), BF),
            pltpu.VMEM((2, 2, 2, 8, 1024), BF),
            pltpu.VMEM((2, 2, 2, 2, 8, 1024), BF),
            pltpu.SMEM((2, 2), jnp.int32),
            dma((7,)), dma((7,)), dma((8,)), dma((8,)), dma((8,)), dma((4,)), dma((4,)),
            dma((7, 2)), dma((8, 2)), dma((1,)), dma((1,)), dma((3, 2)), dma((4, 2)), dma((1,)), dma((2,)),
            dma((3,)), dma((3,)), dma((2, 2)), dma((2, 2)), dma((3,)), dma((3,)),
        ],
        compiler_params=pltpu.CompilerParams(
            collective_id=0, has_side_effects=True, vmem_limit_bytes=60 * 1024 * 1024
        ),
    )(transfers, waves, screened, gmap, coulomb, table())
    r = out.reshape(2, 2, 16, 2, 2, 2, 16)
    first = lax.axis_index("kx") % 2 == 0
    r = jnp.where(first, r[:, :, :, :, 0], r[:, :, :, :, 1])
    direct = r[:, 0].reshape(2, 4, 4, 2, 2, 4, 4).transpose(0, 3, 4, 5, 1, 6, 2)
    exch = r[:, 1].transpose(0, 2, 3, 1, 4)
    return direct.reshape(2, 2, 1, 2, 256), exch.reshape(2, 2, 1, 2, 256)


def solution(mesh):
    return jax.shard_map(
        local,
        mesh=mesh,
        in_specs=(P(None, "kx", "ky", None, None), P(None, None, "kx", None), P(), P(), P()),
        out_specs=(P(None, None, "kx", "ky", None), P(None, None, "kx", "ky", None)),
        check_vma=False,
    )
```

```python
import functools

import jax
import jax.numpy as jnp
import numpy as np
from jax import lax
from jax.experimental import pallas as pl
from jax.experimental.pallas import tpu as pltpu
from jax.sharding import PartitionSpec as P

MESH = pl.DeviceIdType.MESH
OFFS = (0, -1, 1, -2, 2, -3, 3, 4)
BF = jnp.bfloat16
F32 = jnp.float32
NT = (((1,), (1,)), ((), ()))


def table():
    r = np.arange(1024)
    turns = (r[:, None] * r[None, :512]) % 1024
    angles = turns.astype(np.float32) * np.float32(2.0 * np.pi / 1024)
    both = np.concatenate([np.cos(angles), np.sin(angles)], 1)
    return jnp.asarray(both, dtype=BF)


def dot(a, b):
    return lax.dot_general(a, b, (((1,), (0,)), ((), ())), preferred_element_type=F32)


def dot_nt(a, b):
    return lax.dot_general(a, b, NT, preferred_element_type=F32)


def kernel(
    transfers, waves, scr, gmap, coulomb, tab_hbm, out,
    w, hb, tb, lhs, dens, hot, bl, ap, blp, app, yb, zb, res, part,
    tab, gm, cl, eg, vg, fg, xa, xb, tr,
    sem_loc, zs, zr, qs, qr, ys, yr, ss, sr,
    es, er, vs, vr, fs, fr, fas, far, x2s, x2r, bs, br, ps, pr,
):
    kx = lax.axis_index("kx")
    ky = lax.axis_index("ky")
    c = kx % 2
    m = kx // 2
    h = m // 8
    z = m % 8
    y = ky // 2
    xl = ky % 2
    e = y % 2

    def dev(h_, z_, c_, ky_):
        return ((h_ * 8 + z_) * 2 + c_, ky_)

    ky_next, ky_prev = (ky + 1) % 8, (ky + 7) % 8
    m_next, m_prev = (m + 1) % 16, (m + 15) % 16
    other_ky = y * 2 + 1 - xl
    up = dev(h, (z + 1) % 8, c, ky)
    down = dev(h, (z + 7) % 8, c, ky)
    cross = dev(1 - h, z, c, other_ky)
    diag = dev(1 - h, z, 1 - c, other_ky)
    side = dev(h, z, c, other_ky)
    sib = dev(h, z, 1 - c, ky)
    over = dev(1 - h, z, c, ky)
    y_up = dev(h, z, c, (ky + 2) % 8)
    y_down = dev(h, z, c, (ky + 6) % 8)
    next_near, next_far = dev(h, z, c, ky_next), dev(1 - h, z, c, ky_next)
    prev_near, prev_far = dev(h, z, c, ky_prev), dev(1 - h, z, c, ky_prev)
    far_up, far_down = (z + 3) % 8, (z + 5) % 8
    reach = [dev(h, far_up, 0, ky), dev(h, far_down, 0, ky)]
    reach_b = [dev(h, far_up, 1, ky), dev(h, far_down, 1, ky)]
    ahead, behind = (m_next * 2 + 1, ky), (m_prev * 2 + 1, ky)
    last = (jnp.where(c == 0, up[0], down[0]), ky)
    last_y = (kx, jnp.where(c == 0, y_up[1], y_down[1]))
    first = c == 0
    second = c == 1

    own_w = pltpu.make_async_copy(scr.at[c], w.at[:, z, c], sem_loc.at[0])
    own_w.start()
    own_h = pltpu.make_async_copy(waves.at[:, 0], hb.at[c], sem_loc.at[1])
    own_h.start()
    get_tab = pltpu.make_async_copy(tab_hbm, tab, sem_loc.at[2])
    get_tab.start()
    get_gm = pltpu.make_async_copy(gmap, gm, sem_loc.at[3])
    get_gm.start()
    get_cl = pltpu.make_async_copy(coulomb, cl, sem_loc.at[4])
    get_cl.start()
    get_tr = pltpu.make_async_copy(transfers, tr, sem_loc.at[6])
    get_tr.start()

    barrier = pltpu.get_barrier_semaphore()

    def greet(d):
        pl.semaphore_signal(barrier, inc=1, device_id=d, device_id_type=MESH)

    for d in (up, down, cross, diag, side, sib, y_up, y_down, reach[0], reach[1]):
        greet(d)

    @pl.when(first)
    def _():
        for d in (over, next_near, next_far, prev_near, prev_far, reach_b[0], reach_b[1]):
            greet(d)
        pl.semaphore_wait(barrier, 17)

    @pl.when(second)
    def _():
        for d in (ahead, behind):
            greet(d)
        pl.semaphore_wait(barrier, 12)

    ends = {None: [], 0: [], 1: []}

    def send(src, dst, s, r, d, who=None):
        def make():
            return pltpu.make_async_remote_copy(
                src_ref=src(), dst_ref=dst(), send_sem=s(), recv_sem=r(), device_id=d, device_id_type=MESH
            )

        make().start()
        ends[who].append(make)

    def landed(dst, r):
        pltpu.make_async_remote_copy(
            src_ref=dst, dst_ref=dst, send_sem=ss.at[0], recv_sem=r, device_id=sib, device_id_type=MESH
        ).wait_recv()

    def zb_of(k):
        return (z + OFFS[k] + 8) % 8

    def yb_of(k):
        return (y + (0, 3, 1, 2)[k]) % 4

    def f_send(k, p, n, d, k2):
        send(lambda: fg.at[yb_of(k), p], lambda: fg.at[yb_of(k), p], lambda: fs.at[n, p], lambda: fr.at[k2, p], d, 1)

    def f_recv(k, p):
        landed(fg.at[yb_of(k), p], fr.at[k, p])

    @pl.when(second)
    def _():
        send(lambda: waves.at[:, 0], lambda: fg.at[y, 0], lambda: fas.at[0], lambda: far.at[0], ahead, 1)

    send(lambda: waves.at[:, 0], lambda: eg.at[0, c], lambda: es.at[0], lambda: er.at[0, c], reach[0])
    send(lambda: waves.at[:, 0], lambda: eg.at[2, c], lambda: es.at[1], lambda: er.at[2, c], reach[1])

    @pl.when(first)
    def _():
        pltpu.make_async_copy(waves.at[:, 0], eg.at[1, 0], sem_loc.at[5]).start()
        send(lambda: waves.at[:, 0], lambda: fg.at[y, 1], lambda: fas.at[0], lambda: far.at[1], sib, 0)

    @pl.when(second)
    def _():
        send(lambda: waves.at[:, 0], lambda: eg.at[1, 1], lambda: es.at[2], lambda: er.at[1, 1], sib, 1)

    send(lambda: scr.at[1 - c], lambda: w.at[:, z, c], lambda: ss.at[2], lambda: sr.at[2], sib)
    send(lambda: waves.at[:, 0], lambda: hb.at[c], lambda: ss.at[0], lambda: sr.at[0], sib)

    @pl.when(second)
    def _():
        for p in (1, 0):
            landed(fg.at[y, p], far.at[p])
            f_send(0, p, 0, y_up, 1)
            f_send(0, p, 1, y_down, 2)

    def block(k, cc, ri):
        return w.at[ri, zb_of(k), cc]

    def hand(src, sems, there, d):
        send(lambda: src, lambda: src, lambda: sems, lambda: there, d)

    def w_send(k, n, d, k2):
        hand(block(k, e, xl), zs.at[n], zr.at[k2], d)

    def y_way(k):
        return last_y if k == 7 else (y_up if k % 2 == 1 else y_down)

    def w_recv(k):
        landed(block(k, e, xl), zr.at[k])

    def w_spread(k):
        hand(block(k, e, xl), qs.at[k], qr.at[k], side)
        hand(block(k, e, xl), ys.at[k, 0], yr.at[k, 0], y_way(k))

    def s_relay(k):
        landed(block(k, e, 1 - xl), qr.at[k])
        hand(block(k, e, 1 - xl), ys.at[k, 1], yr.at[k, 1], y_way(k))

    own_w.wait()
    landed(w.at[:, z, 1 - c], sr.at[2])
    w_send(0, 0, up, 1)
    w_send(0, 1, down, 2)

    @pl.when(second)
    def _():
        f_recv(1, 0)
        f_send(1, 0, 2, y_up, 3)
        f_recv(2, 1)
        f_send(2, 1, 2, y_down, 3)

    low = lax.broadcasted_iota(jnp.int32, (8, 1024), 0) < 4
    odd = lax.broadcasted_iota(jnp.int32, (8, 1024), 1) % 2 == 1
    sign = jnp.where(odd, F32(-1.0), F32(1.0))
    sign = jnp.concatenate([sign, sign], 0)

    def left(x, at):
        rows = [jnp.broadcast_to(x[at + i : at + i + 1], (8, 1024)) for i in range(4)]
        return jnp.where(low, rows[0], rows[1]), jnp.where(low, rows[2], rows[3])

    def right(x):
        sw = pltpu.roll(x, 4, 0)
        return jnp.where(low, x, sw), jnp.where(low, sw, x)

    def pair(t, q, lr, li, rr, ri):
        re = jnp.concatenate([lr[i] * rr + li[i] * ri for i in (0, 1)], 0)
        im = jnp.concatenate([lr[i] * ri - li[i] * rr for i in (0, 1)], 0)
        if t < 2:
            slot, at, gap = q // 2, t * 64 + (q % 2) * 16, 32
        else:
            slot, at, gap = t, q * 16, 64
        lhs[slot, at : at + 16] = re.astype(BF)
        lhs[slot, at + gap : at + gap + 16] = im.astype(BF)
        lhs[slot, at + 128 : at + 144] = (re * sign).astype(BF)
        lhs[slot, at + gap + 128 : at + gap + 144] = (im * sign).astype(BF)

    def transform(t):
        for g in (0, 1):
            o = dot(lhs[t, g * 128 : g * 128 + 128], tab[...])
            cols = slice(512, 1024) if g == 0 else slice(0, 512)
            dens[t, :64, cols] = (o[:64, :512] + o[64:, 512:]).astype(BF)
            dens[t, 64:, cols] = (o[64:, :512] - o[:64, 512:]).astype(BF)

    own_h.wait()
    landed(hb.at[1 - c], sr.at[0])
    for q in range(4):
        hre = hb[q // 2, 0, q % 2].astype(F32)
        him = hb[q // 2, 1, q % 2].astype(F32)
        pair(2, q, left(hre, 0), left(him, 0), right(hre)[1], right(him)[1])
    get_tab.wait()
    get_tr.wait()
    get_gm.wait()

    def spots_y(own_ky):
        got = []
        for pt in (0, 1):
            g = own_ky * 2 + pt + tr[1, 1]
            ky_t = (g // 2) % 8
            got.append((ky_t // 2, ky_t % 2, g % 2))
        return got

    def spots_x():
        got = []
        for p in (0, 1):
            step = p + tr[0, 0]
            d = (step // 2) % 8
            a = jnp.where(d >= 5, jnp.where(d >= 7, 0, -1), jnp.where(d >= 2, 1, 0))
            b = (d - 3 * a + 9) % 8 - 1
            got.append((((m * 2 + step) % 32) // 16, a + 1, b + 1, step % 2))
        return got

    w_recv(1)
    w_send(1, 2, up, 3)
    w_recv(2)
    w_send(2, 3, down, 4)
    w_spread(1)
    w_spread(2)

    @pl.when(first)
    def _():
        pltpu.make_async_copy(waves.at[:, 0], eg.at[1, 0], sem_loc.at[5]).wait()
        landed(eg.at[1, 1], er.at[1, 1])
        for a in (0, 2):
            for p in (0, 1):
                landed(eg.at[a, p], er.at[a, p])
        for p, (_, a, _, p_t) in enumerate(spots_x()):
            for ri in (0, 1):
                for pt in (0, 1):
                    vg[1, p, ri, pt] = eg[a, p_t, ri, pt]
        send(lambda: vg.at[1], lambda: vg.at[0], lambda: vs.at[0], lambda: vr.at[0], up, 0)
        send(lambda: vg.at[1], lambda: vg.at[2], lambda: vs.at[1], lambda: vr.at[1], down, 0)

    @pl.when(second)
    def _():
        f_recv(1, 1)
        f_recv(2, 0)
        f_recv(3, 0)
        f_recv(3, 1)
        for pt, (y_t, _, p_t) in enumerate(spots_y(other_ky)):
            for p in (0, 1):
                for ri in (0, 1):
                    xa[pt, p, ri] = fg[y_t, p, ri, p_t]
        send(lambda: xa, lambda: xb.at[0], lambda: x2s.at[0], lambda: x2r.at[0], side, 1)

    w_recv(3)
    w_send(3, 4, up, 5)
    w_recv(4)
    w_send(4, 5, down, 6)

    @pl.when(first)
    def _():
        landed(vg.at[0], vr.at[0])
        landed(vg.at[2], vr.at[1])
        for p, (_, _, b, _) in enumerate(spots_x()):
            for ri in (0, 1):
                for pt in (0, 1):
                    xa[pt, p, ri] = vg[b, p, ri, pt]
        send(lambda: xa.at[1], lambda: xb.at[1, 0], lambda: x2s.at[1], lambda: x2r.at[1], next_near, 0)
        send(lambda: xa.at[1], lambda: xb.at[1, 1], lambda: x2s.at[2], lambda: x2r.at[2], next_far, 0)
        send(lambda: xa.at[0], lambda: xb.at[0, 0], lambda: x2s.at[0], lambda: x2r.at[0], over, 0)

    k_last = jnp.where(c == 0, (z + 5) % 8, (z + 3) % 8)
    w_spread(3)
    w_spread(4)
    transform(2)
    w_recv(5)
    w_recv(6)
    hand(w.at[xl, k_last, e], zs.at[6], zr.at[7], last)
    s_relay(1)
    s_relay(2)

    zero = lax.broadcasted_iota(jnp.int32, (8, 1024), 0) * 0

    @pl.when(first)
    def _():
        landed(xb.at[0, 0], x2r.at[0])
        landed(xb.at[1, 0], x2r.at[1])
        landed(xb.at[1, 1], x2r.at[2])
        for p, (h_t, _, _, _) in enumerate(spots_x()):
            near = zero + h_t == h
            for ri in (0, 1):
                tb[p, ri, 1] = jnp.where(near, xa[0, p, ri].astype(F32), xb[0, 0, p, ri].astype(F32)).astype(BF)
                tb[p, ri, 0] = jnp.where(near, xb[1, 0, p, ri].astype(F32), xb[1, 1, p, ri].astype(F32)).astype(BF)

    @pl.when(second)
    def _():
        landed(xb.at[0], x2r.at[0])
        for pt, (y_t, xl_t, p_t) in enumerate(spots_y(ky)):
            near = zero + xl_t == xl
            for p in (0, 1):
                for ri in (0, 1):
                    tb[p, ri, pt] = jnp.where(
                        near, fg[y_t, p, ri, p_t].astype(F32), xb[0, pt, p, ri].astype(F32)
                    ).astype(BF)

    for q in range(4):
        p, pt = q // 2, q % 2
        hre = hb[p, 0, pt].astype(F32)
        him = hb[p, 1, pt].astype(F32)
        tre = tb[p, 0, pt].astype(F32)
        tim = tb[p, 1, pt].astype(F32)
        (trv, trc), (tiv, tic) = right(tre), right(tim)
        pair(0, q, left(hre, 4), left(him, 4), trc, tic)
        pair(1, q, left(hre, 0), left(him, 0), trv, tiv)
        pair(3, q, left(tre, 0), left(tim, 0), trc, tic)


    def transform_ab(p):
        for g in (0, 1):
            o = dot(lhs[p, g * 128 : g * 128 + 128], tab[...])
            cols = slice(512, 1024) if g == 0 else slice(0, 512)
            for t in (0, 1):
                re, im = o[t * 64 : t * 64 + 32], o[t * 64 + 32 : t * 64 + 64]
                dens[t, p * 32 : p * 32 + 32, cols] = (re[:, :512] + im[:, 512:]).astype(BF)
                dens[t, 64 + p * 32 : 96 + p * 32, cols] = (im[:, :512] - re[:, 512:]).astype(BF)

    def permute(q):
        p, pt = q // 2, q % 2
        wx = jnp.where(m * 2 + p + tr[c, 0] >= 32, 1, 0)
        wy = jnp.where(ky * 2 + pt + tr[c, 1] >= 16, 2, 0)
        row = gm[c, pl.ds(wx + wy, 1), :]
        hot[...] = jnp.where(
            lax.broadcasted_iota(jnp.int32, (1024, 1024), 0) == row, F32(1.0), F32(0.0)
        ).astype(BF)
        at = slice(q * 16, q * 16 + 16)
        rows = jnp.concatenate(
            [dens[0, at], dens[0, 64 + q * 16 : 80 + q * 16], dens[1, at], dens[1, 64 + q * 16 : 80 + q * 16]], 0
        )
        o = dot(rows, hot[...]).astype(BF)
        for hh in (0, 1):
            cols = slice(hh * 512, hh * 512 + 512)
            ap[hh, 0, at] = o[0:16, cols]
            ap[hh, 1, at] = o[16:32, cols]
        bl[0, 0, at] = o[32:48]
        bl[0, 1, at] = o[48:64]
        bl[1, 0, at] = -o[48:64]
        bl[1, 1, at] = o[32:48]

    def share(p):
        at = pl.ds(p * 32, 32)
        send(lambda: bl.at[0, :, at], lambda: blp.at[0, :, at], lambda: bs.at[p, 0], lambda: br.at[p, 0], cross)
        send(lambda: ap.at[1 - h, :, at], lambda: app.at[:, at], lambda: bs.at[p, 1], lambda: br.at[p, 1], cross)

    w_spread(5)
    w_spread(6)
    transform_ab(0)
    permute(0)
    permute(1)
    share(0)
    w_recv(7)
    w_spread(7)
    s_relay(3)
    s_relay(4)
    transform_ab(1)
    permute(2)
    permute(3)
    share(1)
    s_relay(5)
    s_relay(6)

    row_q = lax.broadcasted_iota(jnp.int32, (64, 128), 0) // 16
    lane = lax.broadcasted_iota(jnp.int32, (64, 128), 1)
    keep = row_q == (lane % 64) // 16
    flip = jnp.where(lane < 64, F32(1.0), F32(-1.0))

    def fold(d):
        r = d[:64] + flip * pltpu.roll(d[64:], 64, 1)
        r = jnp.where(keep, r, F32(0.0))
        return (r[0:16] + r[16:32]) + (r[32:48] + r[48:64])

    transform(3)
    get_cl.wait()
    zb[...] = (dens[3].astype(F32) * cl[...]).astype(BF)
    res[1] = fold(dot_nt(dens[2], zb[...]))
    send(lambda: res.at[1], lambda: part.at[0, 1], lambda: ps.at[3], lambda: pr.at[3], sib)

    s_relay(7)
    for k in range(1, 8):
        landed(block(k, 1 - e, xl), yr.at[k, 0])
        landed(block(k, 1 - e, 1 - xl), yr.at[k, 1])

    def product(b, a):
        wr = w[0].reshape(512, 1024)
        wi = w[1].reshape(512, 1024)
        yb[...] = (dot_nt(wr, b[0].reshape(128, 1024)) + dot_nt(wi, b[1].reshape(128, 1024))).astype(BF)
        return fold(dot(a.reshape(128, 512), yb[...]))

    res[0] = product(bl, ap[h])
    send(lambda: res.at[0], lambda: part.at[0, 0], lambda: ps.at[0], lambda: pr.at[0], sib)
    for p in (0, 1):
        at = pl.ds(p * 32, 32)
        landed(blp.at[0, :, at], br.at[p, 0])
        landed(app.at[:, at], br.at[p, 1])
    blp[1, 0] = -blp[0, 1]
    blp[1, 1] = blp[0, 0]
    part[3, 0] = product(blp, app[...])
    send(lambda: part.at[3, 0], lambda: part.at[1, 0], lambda: ps.at[1], lambda: pr.at[1], cross)
    send(lambda: part.at[3, 0], lambda: part.at[2, 0], lambda: ps.at[2], lambda: pr.at[2], diag)

    spot = lax.broadcasted_iota(jnp.int32, (128, 1024), 0)
    wide = lax.broadcasted_iota(jnp.int32, (128, 1024), 1)
    lane_l = wide % 256
    base = (wide // 512) * 64 + c * 32 + ((wide // 256) % 2) * 16
    row_l = lax.broadcasted_iota(jnp.int32, (16, 1024), 0)
    wide_l = lax.broadcasted_iota(jnp.int32, (16, 1024), 1) % 256

    def lay(kind, mine, other, col, row):
        both = jnp.concatenate([mine, other], 0)
        pick = jnp.where(spot == base + col, F32(1.0), F32(0.0))
        o = lax.dot_general(
            both, pick, (((1,), (0,)), ((), ())),
            precision=lax.Precision.HIGHEST, preferred_element_type=F32,
        )
        hit = row_l == row
        for i, j in ((0, c), (1, 1 - c)):
            flat = jnp.sum(jnp.where(hit, o[i * 16 : i * 16 + 16], F32(0.0)), 0, keepdims=True)
            for n in range(4):
                out[kind, j, n // 2, 0, n % 2 : n % 2 + 1] = flat[:, n * 256 : n * 256 + 256]

    landed(part.at[0, 1], pr.at[3])
    lay(1, res[1], part[0, 1], lane_l % 16, wide_l // 16)
    landed(part.at[0, 0], pr.at[0])
    landed(part.at[1, 0], pr.at[1])
    landed(part.at[2, 0], pr.at[2])
    lay(
        0, res[0] + part[1, 0], part[0, 0] + part[2, 0],
        (lane_l // 64) * 4 + (lane_l // 4) % 4, ((wide_l // 16) % 4) * 4 + wide_l % 4,
    )
    for make in ends[None]:
        make().wait_send()

    @pl.when(first)
    def _():
        for make in ends[0]:
            make().wait_send()

    @pl.when(second)
    def _():
        for make in ends[1]:
            make().wait_send()


def local(waves, screened, coulomb, transfers, gmap):
    vmem = pl.BlockSpec(memory_space=pltpu.VMEM)
    hbm = pl.BlockSpec(memory_space=pl.ANY)
    dma = pltpu.SemaphoreType.DMA
    out = pl.pallas_call(
        kernel,
        out_shape=jax.ShapeDtypeStruct((2, 2, 2, 1, 2, 256), F32),
        in_specs=[hbm] * 6,
        out_specs=vmem,
        scratch_shapes=[
            pltpu.VMEM((2, 8, 2, 32, 1024), BF),
            pltpu.VMEM((2, 2, 2, 8, 1024), BF),
            pltpu.VMEM((2, 2, 2, 8, 1024), BF),
            pltpu.VMEM((4, 256, 1024), BF),
            pltpu.VMEM((4, 128, 1024), BF),
            pltpu.VMEM((1024, 1024), BF),
            pltpu.VMEM((2, 2, 64, 1024), BF),
            pltpu.VMEM((2, 2, 64, 512), BF),
            pltpu.VMEM((2, 2, 64, 1024), BF),
            pltpu.VMEM((2, 64, 512), BF),
            pltpu.VMEM((512, 128), BF),
            pltpu.VMEM((128, 1024), BF),
            pltpu.VMEM((2, 16, 128), F32),
            pltpu.VMEM((4, 2, 16, 128), F32),
            pltpu.VMEM((1024, 1024), BF),
            pltpu.VMEM((2, 4, 1024), jnp.int32),
            pltpu.VMEM((1024,), F32),
            pltpu.VMEM((3, 2, 2, 2, 8, 1024), BF),
            pltpu.VMEM((3, 2, 2, 2, 8, 1024), BF),
            pltpu.VMEM((4, 2, 2, 2, 8, 1024), BF),
            pltpu.VMEM((2, 2, 2, 8, 1024), BF),
            pltpu.VMEM((2, 2, 2, 2, 8, 1024), BF),
            pltpu.SMEM((2, 2), jnp.int32),
            dma((7,)), dma((7,)), dma((8,)), dma((8,)), dma((8,)), dma((8, 2)), dma((8, 2)), dma((4,)), dma((4,)),
            dma((3,)), dma((3, 2)), dma((2,)), dma((2,)), dma((3, 2)), dma((4, 2)), dma((1,)), dma((2,)),
            dma((3,)), dma((3,)), dma((2, 2)), dma((2, 2)), dma((4,)), dma((4,)),
        ],
        compiler_params=pltpu.CompilerParams(
            collective_id=0, has_side_effects=True, vmem_limit_bytes=60 * 1024 * 1024
        ),
    )(transfers, waves, screened, gmap, coulomb, table())
    return out[0], out[1]


def solution(mesh):
    return jax.shard_map(
        local,
        mesh=mesh,
        in_specs=(P(None, "kx", "ky", None, None), P(None, None, "kx", None), P(), P(), P()),
        out_specs=(P(None, None, "kx", "ky", None), P(None, None, "kx", "ky", None)),
        check_vma=False,
    )
```

```python
import functools

import jax
import jax.numpy as jnp
import numpy as np
from jax import lax
from jax.experimental import pallas as pl
from jax.experimental.pallas import tpu as pltpu
from jax.sharding import PartitionSpec as P

MESH = pl.DeviceIdType.MESH
OFFS = (0, -1, 1, -2, 2, -3, 3, 4)
BF = jnp.bfloat16
F32 = jnp.float32
NT = (((1,), (1,)), ((), ()))


def table():
    r = np.arange(1024)
    turns = (r[:, None] * r[None, :512]) % 1024
    angles = turns.astype(np.float32) * np.float32(2.0 * np.pi / 1024)
    both = np.concatenate([np.cos(angles), np.sin(angles)], 1)
    return jnp.asarray(both, dtype=BF)


def dot(a, b):
    return lax.dot_general(a, b, (((1,), (0,)), ((), ())), preferred_element_type=F32)


def dot_nt(a, b):
    return lax.dot_general(a, b, NT, preferred_element_type=F32)


def kernel(
    transfers, waves, scr, gmap, coulomb, tab_hbm, out,
    w, hb, tb, lhs, dens, hot, bl, ap, hbf, tbf, yb, zb, res, part,
    tab, gm, cl, eg, vg, fg, xa, xb, tr,
    sem_loc, zs, zr, qs, qr, ys, yr, ss, sr,
    es, er, vs, vr, fs, fr, fas, far, x2s, x2r, bs, br, ps, pr,
):
    kx = lax.axis_index("kx")
    ky = lax.axis_index("ky")
    c = kx % 2
    m = kx // 2
    h = m // 8
    z = m % 8
    y = ky // 2
    xl = ky % 2
    e = y % 2

    def dev(h_, z_, c_, ky_):
        return ((h_ * 8 + z_) * 2 + c_, ky_)

    ky_next, ky_prev = (ky + 1) % 8, (ky + 7) % 8
    m_next, m_prev = (m + 1) % 16, (m + 15) % 16
    other_ky = y * 2 + 1 - xl
    up = dev(h, (z + 1) % 8, c, ky)
    down = dev(h, (z + 7) % 8, c, ky)
    cross = dev(1 - h, z, c, other_ky)
    diag = dev(1 - h, z, 1 - c, other_ky)
    side = dev(h, z, c, other_ky)
    sib = dev(h, z, 1 - c, ky)
    over = dev(1 - h, z, c, ky)
    y_up = dev(h, z, c, (ky + 2) % 8)
    y_down = dev(h, z, c, (ky + 6) % 8)
    next_near, next_far = dev(h, z, c, ky_next), dev(1 - h, z, c, ky_next)
    prev_near, prev_far = dev(h, z, c, ky_prev), dev(1 - h, z, c, ky_prev)
    far_up, far_down = (z + 3) % 8, (z + 5) % 8
    reach = [dev(h, far_up, 0, ky), dev(h, far_down, 0, ky)]
    reach_b = [dev(h, far_up, 1, ky), dev(h, far_down, 1, ky)]
    ahead, behind = (m_next * 2 + 1, ky), (m_prev * 2 + 1, ky)
    last = (jnp.where(c == 0, up[0], down[0]), ky)
    last_y = (kx, jnp.where(c == 0, y_up[1], y_down[1]))
    first = c == 0
    second = c == 1

    own_w = pltpu.make_async_copy(scr.at[c], w.at[:, z, c], sem_loc.at[0])
    own_w.start()
    own_h = pltpu.make_async_copy(waves.at[:, 0], hb.at[c], sem_loc.at[1])
    own_h.start()
    get_tab = pltpu.make_async_copy(tab_hbm, tab, sem_loc.at[2])
    get_tab.start()
    get_gm = pltpu.make_async_copy(gmap, gm, sem_loc.at[3])
    get_gm.start()
    get_cl = pltpu.make_async_copy(coulomb, cl, sem_loc.at[4])
    get_cl.start()
    get_tr = pltpu.make_async_copy(transfers, tr, sem_loc.at[6])
    get_tr.start()

    barrier = pltpu.get_barrier_semaphore()

    def greet(d):
        pl.semaphore_signal(barrier, inc=1, device_id=d, device_id_type=MESH)

    for d in (up, down, cross, diag, side, sib, y_up, y_down, reach[0], reach[1]):
        greet(d)

    @pl.when(first)
    def _():
        for d in (over, next_near, next_far, prev_near, prev_far, reach_b[0], reach_b[1]):
            greet(d)
        pl.semaphore_wait(barrier, 17)

    @pl.when(second)
    def _():
        for d in (ahead, behind):
            greet(d)
        pl.semaphore_wait(barrier, 12)

    ends = {None: [], 0: [], 1: []}

    def send(src, dst, s, r, d, who=None):
        def make():
            return pltpu.make_async_remote_copy(
                src_ref=src(), dst_ref=dst(), send_sem=s(), recv_sem=r(), device_id=d, device_id_type=MESH
            )

        make().start()
        ends[who].append(make)

    def landed(dst, r):
        pltpu.make_async_remote_copy(
            src_ref=dst, dst_ref=dst, send_sem=ss.at[0], recv_sem=r, device_id=sib, device_id_type=MESH
        ).wait_recv()

    def zb_of(k):
        return (z + OFFS[k] + 8) % 8

    def yb_of(k):
        return (y + (0, 3, 1, 2)[k]) % 4

    def f_send(k, p, n, d, k2):
        send(lambda: fg.at[yb_of(k), p], lambda: fg.at[yb_of(k), p], lambda: fs.at[n, p], lambda: fr.at[k2, p], d, 1)

    def f_recv(k, p):
        landed(fg.at[yb_of(k), p], fr.at[k, p])

    @pl.when(second)
    def _():
        send(lambda: waves.at[:, 0], lambda: fg.at[y, 0], lambda: fas.at[0], lambda: far.at[0], ahead, 1)

    send(lambda: waves.at[:, 0], lambda: eg.at[0, c], lambda: es.at[0], lambda: er.at[0, c], reach[0])
    send(lambda: waves.at[:, 0], lambda: eg.at[2, c], lambda: es.at[1], lambda: er.at[2, c], reach[1])

    @pl.when(first)
    def _():
        pltpu.make_async_copy(waves.at[:, 0], eg.at[1, 0], sem_loc.at[5]).start()
        send(lambda: waves.at[:, 0], lambda: fg.at[y, 1], lambda: fas.at[0], lambda: far.at[1], sib, 0)

    @pl.when(second)
    def _():
        send(lambda: waves.at[:, 0], lambda: eg.at[1, 1], lambda: es.at[2], lambda: er.at[1, 1], sib, 1)

    send(lambda: scr.at[1 - c], lambda: w.at[:, z, c], lambda: ss.at[2], lambda: sr.at[2], sib)
    send(lambda: waves.at[:, 0], lambda: hbf.at[c], lambda: bs.at[0], lambda: br.at[c], cross)
    send(lambda: waves.at[:, 0], lambda: hbf.at[c], lambda: bs.at[1], lambda: br.at[c], diag)
    send(lambda: waves.at[:, 0], lambda: hb.at[c], lambda: ss.at[0], lambda: sr.at[0], sib)

    @pl.when(second)
    def _():
        for p in (1, 0):
            landed(fg.at[y, p], far.at[p])
            f_send(0, p, 0, y_up, 1)
            f_send(0, p, 1, y_down, 2)

    def block(k, cc, ri):
        return w.at[ri, zb_of(k), cc]

    def hand(src, sems, there, d):
        send(lambda: src, lambda: src, lambda: sems, lambda: there, d)

    def w_send(k, n, d, k2):
        hand(block(k, e, xl), zs.at[n], zr.at[k2], d)

    def y_way(k):
        return last_y if k == 7 else (y_up if k % 2 == 1 else y_down)

    def w_recv(k):
        landed(block(k, e, xl), zr.at[k])

    def w_spread(k):
        hand(block(k, e, xl), qs.at[k], qr.at[k], side)
        hand(block(k, e, xl), ys.at[k, 0], yr.at[k, 0], y_way(k))

    def s_relay(k):
        landed(block(k, e, 1 - xl), qr.at[k])
        hand(block(k, e, 1 - xl), ys.at[k, 1], yr.at[k, 1], y_way(k))

    own_w.wait()
    landed(w.at[:, z, 1 - c], sr.at[2])
    w_send(0, 0, up, 1)
    w_send(0, 1, down, 2)

    @pl.when(second)
    def _():
        f_recv(1, 0)
        f_send(1, 0, 2, y_up, 3)
        f_recv(2, 1)
        f_send(2, 1, 2, y_down, 3)

    low = lax.broadcasted_iota(jnp.int32, (8, 1024), 0) < 4
    odd = lax.broadcasted_iota(jnp.int32, (8, 1024), 1) % 2 == 1
    sign = jnp.where(odd, F32(-1.0), F32(1.0))
    sign = jnp.concatenate([sign, sign], 0)

    def left(x, at):
        rows = [jnp.broadcast_to(x[at + i : at + i + 1], (8, 1024)) for i in range(4)]
        return jnp.where(low, rows[0], rows[1]), jnp.where(low, rows[2], rows[3])

    def right(x):
        sw = pltpu.roll(x, 4, 0)
        return jnp.where(low, x, sw), jnp.where(low, sw, x)

    def pair(t, q, lr, li, rr, ri):
        re = jnp.concatenate([lr[i] * rr + li[i] * ri for i in (0, 1)], 0)
        im = jnp.concatenate([lr[i] * ri - li[i] * rr for i in (0, 1)], 0)
        if t < 2:
            slot, at, gap = q // 2, t * 64 + (q % 2) * 16, 32
        else:
            slot, at, gap = t, q * 16, 64
        lhs[slot, at : at + 16] = re.astype(BF)
        lhs[slot, at + gap : at + gap + 16] = im.astype(BF)
        lhs[slot, at + 128 : at + 144] = (re * sign).astype(BF)
        lhs[slot, at + gap + 128 : at + gap + 144] = (im * sign).astype(BF)

    def transform(t):
        for g in (0, 1):
            o = dot(lhs[t, g * 128 : g * 128 + 128], tab[...])
            cols = slice(512, 1024) if g == 0 else slice(0, 512)
            dens[t, :64, cols] = (o[:64, :512] + o[64:, 512:]).astype(BF)
            dens[t, 64:, cols] = (o[64:, :512] - o[:64, 512:]).astype(BF)

    own_h.wait()
    landed(hb.at[1 - c], sr.at[0])
    for q in range(4):
        hre = hb[q // 2, 0, q % 2].astype(F32)
        him = hb[q // 2, 1, q % 2].astype(F32)
        pair(2, q, left(hre, 0), left(him, 0), right(hre)[1], right(him)[1])
    get_tab.wait()
    get_tr.wait()
    get_gm.wait()

    def spots_y(own_ky):
        got = []
        for pt in (0, 1):
            g = own_ky * 2 + pt + tr[1, 1]
            ky_t = (g // 2) % 8
            got.append((ky_t // 2, ky_t % 2, g % 2))
        return got

    def spots_x():
        got = []
        for p in (0, 1):
            step = p + tr[0, 0]
            d = (step // 2) % 8
            a = jnp.where(d >= 5, jnp.where(d >= 7, 0, -1), jnp.where(d >= 2, 1, 0))
            b = (d - 3 * a + 9) % 8 - 1
            got.append((((m * 2 + step) % 32) // 16, a + 1, b + 1, step % 2))
        return got

    def build(q, far):
        p, pt = q // 2, q % 2
        m_q = (m + 8) % 16 if far else m
        ky_q = other_ky if far else ky
        wx = jnp.where(m_q * 2 + p + tr[c, 0] >= 32, 1, 0)
        wy = jnp.where(ky_q * 2 + pt + tr[c, 1] >= 16, 2, 0)
        row = gm[c, pl.ds(wx + wy, 1), :]
        hot[far * 4 + q] = jnp.where(
            lax.broadcasted_iota(jnp.int32, (1024, 1024), 0) == row, F32(1.0), F32(0.0)
        ).astype(BF)

    for q in range(4):
        build(q, 0)
        build(q, 1)
    w_recv(1)
    w_send(1, 2, up, 3)
    w_recv(2)
    w_send(2, 3, down, 4)
    w_spread(1)
    w_spread(2)

    @pl.when(first)
    def _():
        pltpu.make_async_copy(waves.at[:, 0], eg.at[1, 0], sem_loc.at[5]).wait()
        landed(eg.at[1, 1], er.at[1, 1])
        for a in (0, 2):
            for p in (0, 1):
                landed(eg.at[a, p], er.at[a, p])
        for p, (_, a, _, p_t) in enumerate(spots_x()):
            for ri in (0, 1):
                for pt in (0, 1):
                    vg[1, p, ri, pt] = eg[a, p_t, ri, pt]
        send(lambda: vg.at[1], lambda: vg.at[0], lambda: vs.at[0], lambda: vr.at[0], up, 0)
        send(lambda: vg.at[1], lambda: vg.at[2], lambda: vs.at[1], lambda: vr.at[1], down, 0)

    @pl.when(second)
    def _():
        f_recv(1, 1)
        f_recv(2, 0)
        f_recv(3, 0)
        f_recv(3, 1)
        for pt, (y_t, _, p_t) in enumerate(spots_y(other_ky)):
            for p in (0, 1):
                for ri in (0, 1):
                    xa[pt, p, ri] = fg[y_t, p, ri, p_t]
        send(lambda: xa, lambda: xb.at[0], lambda: x2s.at[0], lambda: x2r.at[0], side, 1)

    w_recv(3)
    w_send(3, 4, up, 5)
    w_recv(4)
    w_send(4, 5, down, 6)

    @pl.when(first)
    def _():
        landed(vg.at[0], vr.at[0])
        landed(vg.at[2], vr.at[1])
        for p, (_, _, b, _) in enumerate(spots_x()):
            for ri in (0, 1):
                for pt in (0, 1):
                    xa[pt, p, ri] = vg[b, p, ri, pt]
        send(lambda: xa.at[1], lambda: xb.at[1, 0], lambda: x2s.at[1], lambda: x2r.at[1], next_near, 0)
        send(lambda: xa.at[1], lambda: xb.at[1, 1], lambda: x2s.at[2], lambda: x2r.at[2], next_far, 0)
        send(lambda: xa.at[0], lambda: xb.at[0, 0], lambda: x2s.at[0], lambda: x2r.at[0], over, 0)

    k_last = jnp.where(c == 0, (z + 5) % 8, (z + 3) % 8)
    w_spread(3)
    w_spread(4)
    transform(2)
    w_recv(5)
    w_recv(6)
    hand(w.at[xl, k_last, e], zs.at[6], zr.at[7], last)
    w_spread(5)
    w_spread(6)
    s_relay(1)
    s_relay(2)

    zero = lax.broadcasted_iota(jnp.int32, (8, 1024), 0) * 0

    @pl.when(first)
    def _():
        landed(xb.at[0, 0], x2r.at[0])
        landed(xb.at[1, 0], x2r.at[1])
        landed(xb.at[1, 1], x2r.at[2])
        for p, (h_t, _, _, _) in enumerate(spots_x()):
            near = zero + h_t == h
            for ri in (0, 1):
                tb[p, ri, 1] = jnp.where(near, xa[0, p, ri].astype(F32), xb[0, 0, p, ri].astype(F32)).astype(BF)
                tb[p, ri, 0] = jnp.where(near, xb[1, 0, p, ri].astype(F32), xb[1, 1, p, ri].astype(F32)).astype(BF)

    @pl.when(second)
    def _():
        landed(xb.at[0], x2r.at[0])
        for pt, (y_t, xl_t, p_t) in enumerate(spots_y(ky)):
            near = zero + xl_t == xl
            for p in (0, 1):
                for ri in (0, 1):
                    tb[p, ri, pt] = jnp.where(
                        near, fg[y_t, p, ri, p_t].astype(F32), xb[0, pt, p, ri].astype(F32)
                    ).astype(BF)

    send(lambda: tb, lambda: tbf, lambda: bs.at[2], lambda: br.at[2], cross)

    def pairs_ab(left_waves, right_waves, with_x):
        for q in range(4):
            p, pt = q // 2, q % 2
            hre = left_waves[p, 0, pt].astype(F32)
            him = left_waves[p, 1, pt].astype(F32)
            tre = right_waves[p, 0, pt].astype(F32)
            tim = right_waves[p, 1, pt].astype(F32)
            (trv, trc), (tiv, tic) = right(tre), right(tim)
            pair(0, q, left(hre, 4), left(him, 4), trc, tic)
            pair(1, q, left(hre, 0), left(him, 0), trv, tiv)
            if with_x:
                pair(3, q, left(tre, 0), left(tim, 0), trc, tic)

    pairs_ab(hb, tb, True)

    def transform_ab(p):
        for g in (0, 1):
            o = dot(lhs[p, g * 128 : g * 128 + 128], tab[...])
            cols = slice(512, 1024) if g == 0 else slice(0, 512)
            for t in (0, 1):
                re, im = o[t * 64 : t * 64 + 32], o[t * 64 + 32 : t * 64 + 64]
                dens[t, p * 32 : p * 32 + 32, cols] = (re[:, :512] + im[:, 512:]).astype(BF)
                dens[t, 64 + p * 32 : 96 + p * 32, cols] = (im[:, :512] - re[:, 512:]).astype(BF)

    def permute(q, far):
        at = slice(q * 16, q * 16 + 16)
        rows = jnp.concatenate(
            [dens[0, at], dens[0, 64 + q * 16 : 80 + q * 16], dens[1, at], dens[1, 64 + q * 16 : 80 + q * 16]], 0
        )
        o = dot(rows, hot[far * 4 + q]).astype(BF)
        for hh in (0, 1):
            cols = slice(hh * 512, hh * 512 + 512)
            ap[far, hh, 0, at] = o[0:16, cols]
            ap[far, hh, 1, at] = o[16:32, cols]
        bl[0, far, 0, at] = o[32:48]
        bl[0, far, 1, at] = o[48:64]
        bl[1, far, 0, at] = -o[48:64]
        bl[1, far, 1, at] = o[32:48]

    transform_ab(0)
    w_recv(7)
    w_spread(7)
    s_relay(3)
    permute(0, 0)
    s_relay(4)
    permute(1, 0)
    transform_ab(1)
    s_relay(5)
    permute(2, 0)
    permute(3, 0)
    s_relay(6)
    row_q = lax.broadcasted_iota(jnp.int32, (64, 128), 0) // 16
    lane = lax.broadcasted_iota(jnp.int32, (64, 128), 1)
    keep = row_q == (lane % 64) // 16
    flip = jnp.where(lane < 64, F32(1.0), F32(-1.0))

    def fold(d):
        r = d[:64] + flip * pltpu.roll(d[64:], 64, 1)
        r = jnp.where(keep, r, F32(0.0))
        return (r[0:16] + r[16:32]) + (r[32:48] + r[48:64])

    transform(3)
    get_cl.wait()
    zb[...] = (dens[3].astype(F32) * cl[...]).astype(BF)
    res[1] = fold(dot_nt(dens[2], zb[...]))
    send(lambda: res.at[1], lambda: part.at[0, 1], lambda: ps.at[3], lambda: pr.at[3], sib)


    landed(hbf.at[0], br.at[0])
    landed(hbf.at[1], br.at[1])
    landed(tbf, br.at[2])
    pairs_ab(hbf, tbf, False)
    transform_ab(0)
    s_relay(7)
    permute(0, 1)
    permute(1, 1)
    transform_ab(1)
    permute(2, 1)
    permute(3, 1)

    for k in range(1, 8):
        landed(block(k, 1 - e, xl), yr.at[k, 0])
        landed(block(k, 1 - e, 1 - xl), yr.at[k, 1])
    wr = w[0].reshape(512, 1024)
    wi = w[1].reshape(512, 1024)
    yb[...] = (dot_nt(wr, bl[0].reshape(256, 1024)) + dot_nt(wi, bl[1].reshape(256, 1024))).astype(BF)
    part[3, 0] = fold(dot(ap[1, h].reshape(128, 512), yb[:, 128:]))
    res[0] = fold(dot(ap[0, h].reshape(128, 512), yb[:, :128]))
    send(lambda: res.at[0], lambda: part.at[0, 0], lambda: ps.at[0], lambda: pr.at[0], sib)
    send(lambda: part.at[3, 0], lambda: part.at[1, 0], lambda: ps.at[1], lambda: pr.at[1], cross)
    send(lambda: part.at[3, 0], lambda: part.at[2, 0], lambda: ps.at[2], lambda: pr.at[2], diag)

    spot = lax.broadcasted_iota(jnp.int32, (128, 1024), 0)
    wide = lax.broadcasted_iota(jnp.int32, (128, 1024), 1)
    lane_l = wide % 256
    base = (wide // 512) * 64 + c * 32 + ((wide // 256) % 2) * 16
    row_l = lax.broadcasted_iota(jnp.int32, (16, 1024), 0)
    wide_l = lax.broadcasted_iota(jnp.int32, (16, 1024), 1) % 256

    def lay(kind, mine, other, col, row):
        both = jnp.concatenate([mine, other], 0)
        pick = jnp.where(spot == base + col, F32(1.0), F32(0.0))
        o = lax.dot_general(
            both, pick, (((1,), (0,)), ((), ())),
            precision=lax.Precision.HIGHEST, preferred_element_type=F32,
        )
        hit = row_l == row
        for i, j in ((0, c), (1, 1 - c)):
            flat = jnp.sum(jnp.where(hit, o[i * 16 : i * 16 + 16], F32(0.0)), 0, keepdims=True)
            for n in range(4):
                out[kind, j, n // 2, 0, n % 2 : n % 2 + 1] = flat[:, n * 256 : n * 256 + 256]

    landed(part.at[0, 1], pr.at[3])
    lay(1, res[1], part[0, 1], lane_l % 16, wide_l // 16)
    landed(part.at[0, 0], pr.at[0])
    landed(part.at[1, 0], pr.at[1])
    landed(part.at[2, 0], pr.at[2])
    lay(
        0, res[0] + part[1, 0], part[0, 0] + part[2, 0],
        (lane_l // 64) * 4 + (lane_l // 4) % 4, ((wide_l // 16) % 4) * 4 + wide_l % 4,
    )
    for make in ends[None]:
        make().wait_send()

    @pl.when(first)
    def _():
        for make in ends[0]:
            make().wait_send()

    @pl.when(second)
    def _():
        for make in ends[1]:
            make().wait_send()


def local(waves, screened, coulomb, transfers, gmap):
    vmem = pl.BlockSpec(memory_space=pltpu.VMEM)
    hbm = pl.BlockSpec(memory_space=pl.ANY)
    dma = pltpu.SemaphoreType.DMA
    out = pl.pallas_call(
        kernel,
        out_shape=jax.ShapeDtypeStruct((2, 2, 2, 1, 2, 256), F32),
        in_specs=[hbm] * 6,
        out_specs=vmem,
        scratch_shapes=[
            pltpu.VMEM((2, 8, 2, 32, 1024), BF),
            pltpu.VMEM((2, 2, 2, 8, 1024), BF),
            pltpu.VMEM((2, 2, 2, 8, 1024), BF),
            pltpu.VMEM((4, 256, 1024), BF),
            pltpu.VMEM((4, 128, 1024), BF),
            pltpu.VMEM((8, 1024, 1024), BF),
            pltpu.VMEM((2, 2, 2, 64, 1024), BF),
            pltpu.VMEM((2, 2, 2, 64, 512), BF),
            pltpu.VMEM((2, 2, 2, 8, 1024), BF),
            pltpu.VMEM((2, 2, 2, 8, 1024), BF),
            pltpu.VMEM((512, 256), BF),
            pltpu.VMEM((128, 1024), BF),
            pltpu.VMEM((2, 16, 128), F32),
            pltpu.VMEM((4, 2, 16, 128), F32),
            pltpu.VMEM((1024, 1024), BF),
            pltpu.VMEM((2, 4, 1024), jnp.int32),
            pltpu.VMEM((1024,), F32),
            pltpu.VMEM((3, 2, 2, 2, 8, 1024), BF),
            pltpu.VMEM((3, 2, 2, 2, 8, 1024), BF),
            pltpu.VMEM((4, 2, 2, 2, 8, 1024), BF),
            pltpu.VMEM((2, 2, 2, 8, 1024), BF),
            pltpu.VMEM((2, 2, 2, 2, 8, 1024), BF),
            pltpu.SMEM((2, 2), jnp.int32),
            dma((7,)), dma((7,)), dma((8,)), dma((8,)), dma((8,)), dma((8, 2)), dma((8, 2)), dma((4,)), dma((4,)),
            dma((3,)), dma((3, 2)), dma((2,)), dma((2,)), dma((3, 2)), dma((4, 2)), dma((1,)), dma((2,)),
            dma((3,)), dma((3,)), dma((3,)), dma((3,)), dma((4,)), dma((4,)),
        ],
        compiler_params=pltpu.CompilerParams(
            collective_id=0, has_side_effects=True, vmem_limit_bytes=60 * 1024 * 1024
        ),
    )(transfers, waves, screened, gmap, coulomb, table())
    return out[0], out[1]


def solution(mesh):
    return jax.shard_map(
        local,
        mesh=mesh,
        in_specs=(P(None, "kx", "ky", None, None), P(None, None, "kx", None), P(), P(), P()),
        out_specs=(P(None, None, "kx", "ky", None), P(None, None, "kx", "ky", None)),
        check_vma=False,
    )
```

```python
import functools

import jax
import jax.numpy as jnp
import numpy as np
from jax import lax
from jax.experimental import pallas as pl
from jax.experimental.pallas import tpu as pltpu
from jax.sharding import PartitionSpec as P

MESH = pl.DeviceIdType.MESH
OFFS = (0, -1, 1, -2, 2, -3, 3, 4)
BF = jnp.bfloat16
F32 = jnp.float32
NT = (((1,), (1,)), ((), ()))


def table():
    r = np.arange(1024)
    turns = (r[:, None] * r[None, :512]) % 1024
    angles = turns.astype(np.float32) * np.float32(2.0 * np.pi / 1024)
    both = np.concatenate([np.cos(angles), np.sin(angles)], 1)
    return jnp.asarray(both, dtype=BF)


def dot(a, b):
    return lax.dot_general(a, b, (((1,), (0,)), ((), ())), preferred_element_type=F32)


def dot_nt(a, b):
    return lax.dot_general(a, b, NT, preferred_element_type=F32)


def kernel(
    transfers, waves, scr, gmap, coulomb, tab_hbm, out,
    w, hb, tb, lhs, dens, hot, bl, ap, hbf, tbf, yb, zb, res, part,
    tab, gm, cl, eg, vg, fg, xa, xb, tr,
    sem_loc, zs, zr, qs, qr, ys, yr, ss, sr,
    es, er, vs, vr, fs, fr, fas, far, x2s, x2r, bs, br, ps, pr,
):
    kx = lax.axis_index("kx")
    ky = lax.axis_index("ky")
    c = kx % 2
    m = kx // 2
    h = m // 8
    z = m % 8
    y = ky // 2
    xl = ky % 2
    e = y % 2

    def dev(h_, z_, c_, ky_):
        return ((h_ * 8 + z_) * 2 + c_, ky_)

    ky_next, ky_prev = (ky + 1) % 8, (ky + 7) % 8
    m_next, m_prev = (m + 1) % 16, (m + 15) % 16
    other_ky = y * 2 + 1 - xl
    up = dev(h, (z + 1) % 8, c, ky)
    down = dev(h, (z + 7) % 8, c, ky)
    cross = dev(1 - h, z, c, other_ky)
    diag = dev(1 - h, z, 1 - c, other_ky)
    side = dev(h, z, c, other_ky)
    sib = dev(h, z, 1 - c, ky)
    over = dev(1 - h, z, c, ky)
    y_up = dev(h, z, c, (ky + 2) % 8)
    y_down = dev(h, z, c, (ky + 6) % 8)
    next_near, next_far = dev(h, z, c, ky_next), dev(1 - h, z, c, ky_next)
    prev_near, prev_far = dev(h, z, c, ky_prev), dev(1 - h, z, c, ky_prev)
    far_up, far_down = (z + 3) % 8, (z + 5) % 8
    reach = [dev(h, far_up, 0, ky), dev(h, far_down, 0, ky)]
    reach_b = [dev(h, far_up, 1, ky), dev(h, far_down, 1, ky)]
    ahead, behind = (m_next * 2 + 1, ky), (m_prev * 2 + 1, ky)
    last = (jnp.where(c == 0, up[0], down[0]), ky)
    last_y = (kx, jnp.where(c == 0, y_up[1], y_down[1]))
    first = c == 0
    second = c == 1

    own_w = pltpu.make_async_copy(scr.at[c], w.at[:, z, c], sem_loc.at[0])
    own_w.start()
    own_h = pltpu.make_async_copy(waves.at[:, 0], hb.at[c], sem_loc.at[1])
    own_h.start()
    get_tab = pltpu.make_async_copy(tab_hbm, tab, sem_loc.at[2])
    get_tab.start()
    get_gm = pltpu.make_async_copy(gmap, gm, sem_loc.at[3])
    get_gm.start()
    get_cl = pltpu.make_async_copy(coulomb, cl, sem_loc.at[4])
    get_cl.start()
    get_tr = pltpu.make_async_copy(transfers, tr, sem_loc.at[6])
    get_tr.start()

    barrier = pltpu.get_barrier_semaphore()

    def greet(d):
        pl.semaphore_signal(barrier, inc=1, device_id=d, device_id_type=MESH)

    for d in (up, down, cross, diag, side, sib, y_up, y_down, reach[0], reach[1]):
        greet(d)

    @pl.when(first)
    def _():
        for d in (over, next_near, next_far, prev_near, prev_far, reach_b[0], reach_b[1]):
            greet(d)
        pl.semaphore_wait(barrier, 17)

    @pl.when(second)
    def _():
        for d in (ahead, behind):
            greet(d)
        pl.semaphore_wait(barrier, 12)

    ends = {None: [], 0: [], 1: []}

    def send(src, dst, s, r, d, who=None):
        def make():
            return pltpu.make_async_remote_copy(
                src_ref=src(), dst_ref=dst(), send_sem=s(), recv_sem=r(), device_id=d, device_id_type=MESH
            )

        make().start()
        ends[who].append(make)

    def landed(dst, r):
        pltpu.make_async_remote_copy(
            src_ref=dst, dst_ref=dst, send_sem=ss.at[0], recv_sem=r, device_id=sib, device_id_type=MESH
        ).wait_recv()

    def zb_of(k):
        return (z + OFFS[k] + 8) % 8

    def yb_of(k):
        return (y + (0, 3, 1, 2)[k]) % 4

    def f_send(k, p, n, d, k2):
        send(lambda: fg.at[yb_of(k), p], lambda: fg.at[yb_of(k), p], lambda: fs.at[n, p], lambda: fr.at[k2, p], d, 1)

    def f_recv(k, p):
        landed(fg.at[yb_of(k), p], fr.at[k, p])

    @pl.when(second)
    def _():
        send(lambda: waves.at[:, 0], lambda: fg.at[y, 0], lambda: fas.at[0], lambda: far.at[0], ahead, 1)

    send(lambda: waves.at[:, 0], lambda: eg.at[0, c], lambda: es.at[0], lambda: er.at[0, c], reach[0])
    send(lambda: waves.at[:, 0], lambda: eg.at[2, c], lambda: es.at[1], lambda: er.at[2, c], reach[1])

    @pl.when(first)
    def _():
        pltpu.make_async_copy(waves.at[:, 0], eg.at[1, 0], sem_loc.at[5]).start()
        send(lambda: waves.at[:, 0], lambda: fg.at[y, 1], lambda: fas.at[0], lambda: far.at[1], sib, 0)

    @pl.when(second)
    def _():
        send(lambda: waves.at[:, 0], lambda: eg.at[1, 1], lambda: es.at[2], lambda: er.at[1, 1], sib, 1)

    send(lambda: scr.at[1 - c], lambda: w.at[:, z, c], lambda: ss.at[2], lambda: sr.at[2], sib)
    send(lambda: waves.at[:, 0], lambda: hbf.at[c], lambda: bs.at[0], lambda: br.at[c], cross)
    send(lambda: waves.at[:, 0], lambda: hbf.at[c], lambda: bs.at[1], lambda: br.at[c], diag)
    send(lambda: waves.at[:, 0], lambda: hb.at[c], lambda: ss.at[0], lambda: sr.at[0], sib)

    @pl.when(second)
    def _():
        for p in (1, 0):
            landed(fg.at[y, p], far.at[p])
            f_send(0, p, 0, y_up, 1)
            f_send(0, p, 1, y_down, 2)

    def block(k, cc, ri):
        return w.at[ri, zb_of(k), cc]

    def hand(src, sems, there, d):
        send(lambda: src, lambda: src, lambda: sems, lambda: there, d)

    def w_send(k, n, d, k2):
        hand(block(k, e, xl), zs.at[n], zr.at[k2], d)

    def y_way(k):
        return last_y if k == 7 else (y_up if k % 2 == 1 else y_down)

    def w_recv(k):
        landed(block(k, e, xl), zr.at[k])

    def w_spread(k):
        hand(block(k, e, xl), qs.at[k], qr.at[k], side)
        hand(block(k, e, xl), ys.at[k, 0], yr.at[k, 0], y_way(k))

    def s_relay(k):
        landed(block(k, e, 1 - xl), qr.at[k])
        hand(block(k, e, 1 - xl), ys.at[k, 1], yr.at[k, 1], y_way(k))

    own_w.wait()
    landed(w.at[:, z, 1 - c], sr.at[2])
    w_send(0, 0, up, 1)
    w_send(0, 1, down, 2)

    @pl.when(second)
    def _():
        f_recv(1, 0)
        f_send(1, 0, 2, y_up, 3)
        f_recv(2, 1)
        f_send(2, 1, 2, y_down, 3)

    low = lax.broadcasted_iota(jnp.int32, (8, 1024), 0) < 4
    odd = lax.broadcasted_iota(jnp.int32, (8, 1024), 1) % 2 == 1
    sign = jnp.where(odd, F32(-1.0), F32(1.0))
    sign = jnp.concatenate([sign, sign], 0)

    def left(x, at):
        rows = [jnp.broadcast_to(x[at + i : at + i + 1], (8, 1024)) for i in range(4)]
        return jnp.where(low, rows[0], rows[1]), jnp.where(low, rows[2], rows[3])

    def right(x):
        sw = pltpu.roll(x, 4, 0)
        return jnp.where(low, x, sw), jnp.where(low, sw, x)

    def pair(t, q, lr, li, rr, ri):
        re = jnp.concatenate([lr[i] * rr + li[i] * ri for i in (0, 1)], 0)
        im = jnp.concatenate([lr[i] * ri - li[i] * rr for i in (0, 1)], 0)
        if t < 2:
            slot, at, gap = q // 2, t * 64 + (q % 2) * 16, 32
        else:
            slot, at, gap = t, q * 16, 64
        lhs[slot, at : at + 16] = re.astype(BF)
        lhs[slot, at + gap : at + gap + 16] = im.astype(BF)
        lhs[slot, at + 128 : at + 144] = (re * sign).astype(BF)
        lhs[slot, at + gap + 128 : at + gap + 144] = (im * sign).astype(BF)

    def transform(t):
        for g in (0, 1):
            o = dot(lhs[t, g * 128 : g * 128 + 128], tab[...])
            cols = slice(512, 1024) if g == 0 else slice(0, 512)
            dens[t, :64, cols] = (o[:64, :512] + o[64:, 512:]).astype(BF)
            dens[t, 64:, cols] = (o[64:, :512] - o[:64, 512:]).astype(BF)

    own_h.wait()
    landed(hb.at[1 - c], sr.at[0])
    for q in range(4):
        hre = hb[q // 2, 0, q % 2].astype(F32)
        him = hb[q // 2, 1, q % 2].astype(F32)
        pair(2, q, left(hre, 0), left(him, 0), right(hre)[1], right(him)[1])
    get_tab.wait()
    get_tr.wait()
    get_gm.wait()

    def spots_y(own_ky):
        got = []
        for pt in (0, 1):
            g = own_ky * 2 + pt + tr[1, 1]
            ky_t = (g // 2) % 8
            got.append((ky_t // 2, ky_t % 2, g % 2))
        return got

    def spots_x():
        got = []
        for p in (0, 1):
            step = p + tr[0, 0]
            d = (step // 2) % 8
            a = jnp.where(d >= 5, jnp.where(d >= 7, 0, -1), jnp.where(d >= 2, 1, 0))
            b = (d - 3 * a + 9) % 8 - 1
            got.append((((m * 2 + step) % 32) // 16, a + 1, b + 1, step % 2))
        return got

    def build(q, far):
        p, pt = q // 2, q % 2
        m_q = (m + 8) % 16 if far else m
        ky_q = other_ky if far else ky
        wx = jnp.where(m_q * 2 + p + tr[c, 0] >= 32, 1, 0)
        wy = jnp.where(ky_q * 2 + pt + tr[c, 1] >= 16, 2, 0)
        row = gm[c, pl.ds(wx + wy, 1), :]
        hot[far * 4 + q] = jnp.where(
            lax.broadcasted_iota(jnp.int32, (1024, 1024), 0) == row, F32(1.0), F32(0.0)
        ).astype(BF)

    for q in range(4):
        build(q, 0)
        build(q, 1)
    w_recv(1)
    w_send(1, 2, up, 3)
    w_recv(2)
    w_send(2, 3, down, 4)
    w_spread(1)
    w_spread(2)

    @pl.when(first)
    def _():
        pltpu.make_async_copy(waves.at[:, 0], eg.at[1, 0], sem_loc.at[5]).wait()
        landed(eg.at[1, 1], er.at[1, 1])
        for a in (0, 2):
            for p in (0, 1):
                landed(eg.at[a, p], er.at[a, p])
        for p, (_, a, _, p_t) in enumerate(spots_x()):
            for ri in (0, 1):
                for pt in (0, 1):
                    vg[1, p, ri, pt] = eg[a, p_t, ri, pt]
        send(lambda: vg.at[1], lambda: vg.at[0], lambda: vs.at[0], lambda: vr.at[0], up, 0)
        send(lambda: vg.at[1], lambda: vg.at[2], lambda: vs.at[1], lambda: vr.at[1], down, 0)

    @pl.when(second)
    def _():
        f_recv(1, 1)
        f_recv(2, 0)
        f_recv(3, 0)
        f_recv(3, 1)
        for pt, (y_t, _, p_t) in enumerate(spots_y(other_ky)):
            for p in (0, 1):
                for ri in (0, 1):
                    xa[pt, p, ri] = fg[y_t, p, ri, p_t]
        send(lambda: xa, lambda: xb.at[0], lambda: x2s.at[0], lambda: x2r.at[0], side, 1)

    w_recv(3)
    w_send(3, 4, up, 5)
    w_recv(4)
    w_send(4, 5, down, 6)

    @pl.when(first)
    def _():
        landed(vg.at[0], vr.at[0])
        landed(vg.at[2], vr.at[1])
        for p, (_, _, b, _) in enumerate(spots_x()):
            for ri in (0, 1):
                for pt in (0, 1):
                    xa[pt, p, ri] = vg[b, p, ri, pt]
        send(lambda: xa.at[1], lambda: xb.at[1, 0], lambda: x2s.at[1], lambda: x2r.at[1], next_near, 0)
        send(lambda: xa.at[1], lambda: xb.at[1, 1], lambda: x2s.at[2], lambda: x2r.at[2], next_far, 0)
        send(lambda: xa.at[0], lambda: xb.at[0, 0], lambda: x2s.at[0], lambda: x2r.at[0], over, 0)

    k_last = jnp.where(c == 0, (z + 5) % 8, (z + 3) % 8)
    w_spread(3)
    w_spread(4)
    transform(2)
    w_recv(5)
    w_recv(6)
    hand(w.at[xl, k_last, e], zs.at[6], zr.at[7], last)
    w_spread(5)
    w_spread(6)
    s_relay(1)
    s_relay(2)

    zero = lax.broadcasted_iota(jnp.int32, (8, 1024), 0) * 0

    @pl.when(first)
    def _():
        landed(xb.at[0, 0], x2r.at[0])
        landed(xb.at[1, 0], x2r.at[1])
        landed(xb.at[1, 1], x2r.at[2])
        for p, (h_t, _, _, _) in enumerate(spots_x()):
            near = zero + h_t == h
            for ri in (0, 1):
                tb[p, ri, 1] = jnp.where(near, xa[0, p, ri].astype(F32), xb[0, 0, p, ri].astype(F32)).astype(BF)
                tb[p, ri, 0] = jnp.where(near, xb[1, 0, p, ri].astype(F32), xb[1, 1, p, ri].astype(F32)).astype(BF)

    @pl.when(second)
    def _():
        landed(xb.at[0], x2r.at[0])
        for pt, (y_t, xl_t, p_t) in enumerate(spots_y(ky)):
            near = zero + xl_t == xl
            for p in (0, 1):
                for ri in (0, 1):
                    tb[p, ri, pt] = jnp.where(
                        near, fg[y_t, p, ri, p_t].astype(F32), xb[0, pt, p, ri].astype(F32)
                    ).astype(BF)

    send(lambda: tb, lambda: tbf, lambda: bs.at[2], lambda: br.at[2], cross)

    def pairs_ab(left_waves, right_waves, with_x):
        for q in range(4):
            p, pt = q // 2, q % 2
            hre = left_waves[p, 0, pt].astype(F32)
            him = left_waves[p, 1, pt].astype(F32)
            tre = right_waves[p, 0, pt].astype(F32)
            tim = right_waves[p, 1, pt].astype(F32)
            (trv, trc), (tiv, tic) = right(tre), right(tim)
            pair(0, q, left(hre, 4), left(him, 4), trc, tic)
            pair(1, q, left(hre, 0), left(him, 0), trv, tiv)
            if with_x:
                pair(3, q, left(tre, 0), left(tim, 0), trc, tic)

    pairs_ab(hb, tb, True)

    def transform_ab(p):
        for g in (0, 1):
            o = dot(lhs[p, g * 128 : g * 128 + 128], tab[...])
            cols = slice(512, 1024) if g == 0 else slice(0, 512)
            for t in (0, 1):
                re, im = o[t * 64 : t * 64 + 32], o[t * 64 + 32 : t * 64 + 64]
                dens[t, p * 32 : p * 32 + 32, cols] = (re[:, :512] + im[:, 512:]).astype(BF)
                dens[t, 64 + p * 32 : 96 + p * 32, cols] = (im[:, :512] - re[:, 512:]).astype(BF)

    def permute(q, far):
        at = slice(q * 16, q * 16 + 16)
        rows = jnp.concatenate(
            [dens[0, at], dens[0, 64 + q * 16 : 80 + q * 16], dens[1, at], dens[1, 64 + q * 16 : 80 + q * 16]], 0
        )
        o = dot(rows, hot[far * 4 + q]).astype(BF)
        for hh in (0, 1):
            cols = slice(hh * 512, hh * 512 + 512)
            ap[far, hh, 0, at] = o[0:16, cols]
            ap[far, hh, 1, at] = o[16:32, cols]
        bl[0, far, 0, at] = o[32:48]
        bl[0, far, 1, at] = o[48:64]
        bl[1, far, 0, at] = -o[48:64]
        bl[1, far, 1, at] = o[32:48]

    transform_ab(0)
    w_recv(7)
    w_spread(7)
    s_relay(3)
    permute(0, 0)
    s_relay(4)
    permute(1, 0)
    transform_ab(1)
    s_relay(5)
    permute(2, 0)
    permute(3, 0)
    s_relay(6)
    row_q = lax.broadcasted_iota(jnp.int32, (64, 128), 0) // 16
    lane = lax.broadcasted_iota(jnp.int32, (64, 128), 1)
    keep = row_q == (lane % 64) // 16
    flip = jnp.where(lane < 64, F32(1.0), F32(-1.0))

    def fold(d):
        r = d[:64] + flip * pltpu.roll(d[64:], 64, 1)
        r = jnp.where(keep, r, F32(0.0))
        return (r[0:16] + r[16:32]) + (r[32:48] + r[48:64])

    transform(3)
    get_cl.wait()
    zb[...] = (dens[3].astype(F32) * cl[...]).astype(BF)
    res[1] = fold(dot_nt(dens[2], zb[...]))
    send(lambda: res.at[1], lambda: part.at[0, 1], lambda: ps.at[3], lambda: pr.at[3], sib)


    landed(hbf.at[0], br.at[0])
    landed(hbf.at[1], br.at[1])
    landed(tbf, br.at[2])
    pairs_ab(hbf, tbf, False)
    transform_ab(0)
    s_relay(7)
    permute(0, 1)
    permute(1, 1)
    transform_ab(1)
    permute(2, 1)
    permute(3, 1)

    for k in range(1, 8):
        landed(block(k, 1 - e, xl), yr.at[k, 0])
        landed(block(k, 1 - e, 1 - xl), yr.at[k, 1])
    wr = w[0].reshape(512, 1024)
    wi = w[1].reshape(512, 1024)
    yb[...] = (dot_nt(wr, bl[0].reshape(256, 1024)) + dot_nt(wi, bl[1].reshape(256, 1024))).astype(BF)
    part[3, 0] = fold(dot(ap[1, h].reshape(128, 512), yb[:, 128:]))
    res[0] = fold(dot(ap[0, h].reshape(128, 512), yb[:, :128]))
    send(lambda: res.at[0], lambda: part.at[0, 0], lambda: ps.at[0], lambda: pr.at[0], sib)
    send(lambda: part.at[3, 0], lambda: part.at[1, 0], lambda: ps.at[1], lambda: pr.at[1], cross)
    send(lambda: part.at[3, 0], lambda: part.at[2, 0], lambda: ps.at[2], lambda: pr.at[2], diag)

    spot = lax.broadcasted_iota(jnp.int32, (128, 1024), 0)
    wide = lax.broadcasted_iota(jnp.int32, (128, 1024), 1)
    lane_l = wide % 256
    base = (wide // 512) * 64 + c * 32 + ((wide // 256) % 2) * 16
    row_l = lax.broadcasted_iota(jnp.int32, (16, 1024), 0)
    wide_l = lax.broadcasted_iota(jnp.int32, (16, 1024), 1) % 256

    def lay(kind, mine, other, col, row):
        both = jnp.concatenate([mine, other], 0)
        pick = jnp.where(spot == base + col, F32(1.0), F32(0.0))
        o = lax.dot_general(
            both, pick, (((1,), (0,)), ((), ())),
            precision=lax.Precision.HIGHEST, preferred_element_type=F32,
        )
        hit = row_l == row
        for i, j in ((0, c), (1, 1 - c)):
            flat = jnp.sum(jnp.where(hit, o[i * 16 : i * 16 + 16], F32(0.0)), 0, keepdims=True)
            for n in range(4):
                out[kind, j, n // 2, 0, n % 2 : n % 2 + 1] = flat[:, n * 256 : n * 256 + 256]

    landed(part.at[0, 1], pr.at[3])
    lay(1, res[1], part[0, 1], lane_l % 16, wide_l // 16)
    for make in ends[None]:
        make().wait_send()

    @pl.when(first)
    def _():
        for make in ends[0]:
            make().wait_send()

    @pl.when(second)
    def _():
        for make in ends[1]:
            make().wait_send()

    landed(part.at[0, 0], pr.at[0])
    landed(part.at[1, 0], pr.at[1])
    landed(part.at[2, 0], pr.at[2])
    lay(
        0, res[0] + part[1, 0], part[0, 0] + part[2, 0],
        (lane_l // 64) * 4 + (lane_l // 4) % 4, ((wide_l // 16) % 4) * 4 + wide_l % 4,
    )


def local(waves, screened, coulomb, transfers, gmap):
    vmem = pl.BlockSpec(memory_space=pltpu.VMEM)
    hbm = pl.BlockSpec(memory_space=pl.ANY)
    dma = pltpu.SemaphoreType.DMA
    out = pl.pallas_call(
        kernel,
        out_shape=jax.ShapeDtypeStruct((2, 2, 2, 1, 2, 256), F32),
        in_specs=[hbm] * 6,
        out_specs=vmem,
        scratch_shapes=[
            pltpu.VMEM((2, 8, 2, 32, 1024), BF),
            pltpu.VMEM((2, 2, 2, 8, 1024), BF),
            pltpu.VMEM((2, 2, 2, 8, 1024), BF),
            pltpu.VMEM((4, 256, 1024), BF),
            pltpu.VMEM((4, 128, 1024), BF),
            pltpu.VMEM((8, 1024, 1024), BF),
            pltpu.VMEM((2, 2, 2, 64, 1024), BF),
            pltpu.VMEM((2, 2, 2, 64, 512), BF),
            pltpu.VMEM((2, 2, 2, 8, 1024), BF),
            pltpu.VMEM((2, 2, 2, 8, 1024), BF),
            pltpu.VMEM((512, 256), BF),
            pltpu.VMEM((128, 1024), BF),
            pltpu.VMEM((2, 16, 128), F32),
            pltpu.VMEM((4, 2, 16, 128), F32),
            pltpu.VMEM((1024, 1024), BF),
            pltpu.VMEM((2, 4, 1024), jnp.int32),
            pltpu.VMEM((1024,), F32),
            pltpu.VMEM((3, 2, 2, 2, 8, 1024), BF),
            pltpu.VMEM((3, 2, 2, 2, 8, 1024), BF),
            pltpu.VMEM((4, 2, 2, 2, 8, 1024), BF),
            pltpu.VMEM((2, 2, 2, 8, 1024), BF),
            pltpu.VMEM((2, 2, 2, 2, 8, 1024), BF),
            pltpu.SMEM((2, 2), jnp.int32),
            dma((7,)), dma((7,)), dma((8,)), dma((8,)), dma((8,)), dma((8, 2)), dma((8, 2)), dma((4,)), dma((4,)),
            dma((3,)), dma((3, 2)), dma((2,)), dma((2,)), dma((3, 2)), dma((4, 2)), dma((1,)), dma((2,)),
            dma((3,)), dma((3,)), dma((3,)), dma((3,)), dma((4,)), dma((4,)),
        ],
        compiler_params=pltpu.CompilerParams(
            collective_id=0, has_side_effects=True, vmem_limit_bytes=60 * 1024 * 1024
        ),
    )(transfers, waves, screened, gmap, coulomb, table())
    return out[0], out[1]


def solution(mesh):
    return jax.shard_map(
        local,
        mesh=mesh,
        in_specs=(P(None, "kx", "ky", None, None), P(None, None, "kx", None), P(), P(), P()),
        out_specs=(P(None, None, "kx", "ky", None), P(None, None, "kx", "ky", None)),
        check_vma=False,
    )
```
